32 devices in a mesh: grp: 2 (over x), tile: 16 (over z, y, core).
Axes of the slice: x: 2, y: 2, z: 4, core: 2. Of those that a mesh axis runs over, the one named last changes fastest.
Arguments:
- prognostic: float32 [4, 64, 256, 256], P(None, None, 'tile'), may hold values from 0.2 to 2
- courant: float32 [2, 64, 256, 256], P(None, None, 'tile'), may hold values from -0.22 to 0.22
- daylit: int32 [16384], P('tile'), may hold values from 0 to 1, as said below
- cos_zenith: float32 [16384], P('tile'), may hold values from 0.05 to 1
- albedo: float32 [16384], P('tile'), may hold values from 0.05 to 0.8
- layer_mass: float32 [64], replicated, may hold values from 0.5 to 2
- vapour_absorption: float32 [64, 32], replicated, may hold values from 0.002 to 0.1
- ozone_absorption: float32 [32], replicated, may hold values from 0.002 to 0.1
- cloud_extinction: float32 [32], replicated, may hold values from 0.005 to 0.1
- cloud_albedo: float32 [32], replicated, may hold values from 0.5 to 0.95
- solar_weight: float32 [32], replicated, may hold values from 0.01 to 0.06
Outputs:
- stepped: float32 [2, 4, 64, 256, 256], P('grp', None, None, 'tile')
The draws below stay inside these ranges and needn't reach their ends.
Inputs may be any that keep to these rules, and one draw needn't show every extreme that they name: In all, exactly 8192 coarse columns are daylit.
All inputs are finite; a program needn't handle non-finite values.
Results may differ from the reference program's by a relative error of at most 0.00002.
Values sent between devices are 32-bit elements; how exact they have to be, the bound alone decides.
A program may use at most 256 MiB of HBM per device.

```python
import math
import jax
import jax.numpy as jnp
from jax import lax

G = 32
LEV = 64
COARSEN = 4
NX = 256
NY = 256
CCOL = 1024
NCOARSE = 16384
N_TILE = 16


def draw_daylit(key, part):
    coarse_x = NCOARSE // NY
    subsolar = jax.random.randint(jax.random.fold_in(key, 11), (), 0, coarse_x)
    tilt = jax.random.randint(jax.random.fold_in(key, 12), (), coarse_x // 8, coarse_x // 2 + 1)
    season = 2 * jax.random.randint(jax.random.fold_in(key, 13), (), 0, 2) - 1
    column = jnp.arange(NCOARSE, dtype=jnp.int32)
    lon_index = column // NY
    lat_index = column % NY
    apart = (lon_index - subsolar) % coarse_x
    distance = jnp.minimum(apart, coarse_x - apart)
    score = 2 * NY * distance - season * tilt * (2 * lat_index - NY + 1)
    order = jnp.argsort(score, stable=True)
    return jnp.zeros((NCOARSE,), jnp.int32).at[order[:NCOARSE // 2]].set(1)


def level_of(rng, shape, pieces, low, high):
    def one(dim, shards_of):
        steps = jax.random.uniform(jax.random.fold_in(jax.random.fold_in(rng, 6), dim), (shards_of,), jnp.float32, low / len(pieces), high / len(pieces))
        return jnp.repeat(jnp.exp(steps), shape[dim] // shards_of).reshape((-1,) + (1,) * (len(shape) - dim - 1))

    factor_of = one(*pieces[0])
    for cut in pieces[1:]:
        factor_of = factor_of * one(*cut)
    return factor_of


def setup_inputs(seed: int = 0) -> dict:
    seeds = jax.random.split(jax.random.key(seed), 12)
    return {
        "prognostic": jnp.clip(jnp.exp(math.log(2.0) - 2.3025851 * jax.random.uniform(seeds[0], (4, LEV, NX, NY), jnp.float32) ** level_of(seeds[0], (4, LEV, NX, NY), ((2, 16),), -0.2, 0.2)), 0.2, 2.0),
        "courant": jnp.clip(jax.random.uniform(seeds[1], (2, LEV, NX, NY), jnp.float32, -0.22, 0.22) * level_of(seeds[1], (2, LEV, NX, NY), ((2, 16),), -0.4, 0.0), -0.22, 0.22),
        "daylit": draw_daylit(jax.random.fold_in(seeds[11], 71), 0),
        "cos_zenith": jnp.clip(jnp.exp(math.log(1.0) - 2.9957323 * jax.random.uniform(seeds[3], (NCOARSE,), jnp.float32) ** level_of(seeds[3], (NCOARSE,), ((0, 16),), -0.2, 0.2)), 0.05, 1.0),
        "albedo": jnp.clip(0.05 + 0.75 * jax.random.uniform(seeds[4], (NCOARSE,), jnp.float32) ** level_of(seeds[4], (NCOARSE,), ((0, 16),), -0.2, 0.2), 0.05, 0.8),
        "layer_mass": jnp.clip(jnp.exp(jax.random.uniform(seeds[5], (LEV,), jnp.float32, math.log(0.5), math.log(2.0))), 0.5, 2.0),
        "vapour_absorption": jnp.clip(jnp.exp(jax.random.uniform(seeds[6], (LEV, G), jnp.float32, math.log(0.002), math.log(0.1))), 0.002, 0.1),
        "ozone_absorption": jnp.clip(jnp.exp(jax.random.uniform(seeds[7], (G,), jnp.float32, math.log(0.002), math.log(0.1))), 0.002, 0.1),
        "cloud_extinction": jnp.clip(jnp.exp(jax.random.uniform(seeds[8], (G,), jnp.float32, math.log(0.005), math.log(0.1))), 0.005, 0.1),
        "cloud_albedo": jnp.clip(jax.random.uniform(seeds[9], (G,), jnp.float32, 0.5, 0.95), 0.5, 0.95),
        "solar_weight": jnp.clip(jnp.exp(jax.random.uniform(seeds[10], (G,), jnp.float32, math.log(0.01), math.log(0.06))), 0.01, 0.06),
    }


DIFFUSIVITY = 1.66
STEP_LENGTH = 1.0


def upwind(left_cell, right_cell, courant_face):
    return jnp.maximum(courant_face, 0.0) * left_cell + jnp.minimum(courant_face, 0.0) * right_cell


def donor(padded, face_x, face_y):
    centre = padded[:, :, 1:-1]
    flux_x = upwind(padded[:, :, :-1], padded[:, :, 1:], face_x)
    lower_cell = jnp.concatenate([centre[..., :1], centre[..., :-1]], axis=-1)
    flux_low = upwind(lower_cell, centre, face_y)
    flux_high = jnp.concatenate([flux_low[..., 1:], jnp.zeros_like(flux_low[..., :1])], axis=-1)
    return centre - (flux_x[:, :, 1:] - flux_x[:, :, :-1]) - (flux_high - flux_low)


def corrective(padded, face_x, face_y):
    centre = padded[:, :, 1:-1]
    left_cell = padded[:, :, :-1]
    right_cell = padded[:, :, 1:]
    speed_x = (jnp.abs(face_x) - face_x * face_x) * (right_cell - left_cell) / (right_cell + left_cell)
    lower_cell = jnp.concatenate([centre[..., :1], centre[..., :-1]], axis=-1)
    speed_y = (jnp.abs(face_y) - face_y * face_y) * (centre - lower_cell) / (centre + lower_cell)
    return speed_x, speed_y


def shortwave(profiles, cosine, ground_albedo, layer_mass, vapour_absorption, ozone_absorption, cloud_extinction, cloud_albedo, solar_weight):
    mass_col = layer_mass[:, None, None]
    gas_depth = (vapour_absorption[:, :, None] * profiles[0][:, None, :] + ozone_absorption[None, :, None] * profiles[2][:, None, :]) * mass_col
    cloud_depth = cloud_extinction[None, :, None] * profiles[1][:, None, :] * mass_col
    optical_depth = gas_depth + cloud_depth
    single = cloud_albedo[None, :, None] * cloud_depth / optical_depth
    trans_dir = jnp.exp(-optical_depth / cosine[None, None, :])
    trans_dif = jnp.exp(-DIFFUSIVITY * optical_depth)
    refl_dif = 0.5 * single * (1.0 - trans_dif * trans_dif)
    scat_dir = 0.5 * single * (1.0 - trans_dir)
    ground = jnp.broadcast_to(ground_albedo[None, :], trans_dir.shape[1:])

    def upward(state_pair, layer_terms):
        alb_dif, alb_dir = state_pair
        t_dir, t_dif, r_dif, s_dir = layer_terms
        inverse_den = 1.0 / (1.0 - r_dif * alb_dif)
        down_dif = (s_dir + r_dif * alb_dir * t_dir) * inverse_den
        new_dir = s_dir + t_dif * (alb_dif * down_dif + alb_dir * t_dir)
        new_dif = r_dif + t_dif * t_dif * alb_dif * inverse_den
        return (new_dif, new_dir), (alb_dif, alb_dir, inverse_den)

    (top_dif, top_dir), (below_dif, below_dir, inverse_den) = lax.scan(
        upward, (ground, ground), (trans_dir, trans_dif, refl_dif, scat_dir), reverse=True)
    incoming = solar_weight[:, None] * cosine[None, :]

    def downward(state_pair, layer_terms):
        direct, diffuse = state_pair
        t_dir, t_dif, r_dif, s_dir, alb_dif, alb_dir, den_layer = layer_terms
        direct_low = direct * t_dir
        diffuse_low = (diffuse * t_dif + direct * s_dir + r_dif * alb_dir * direct_low) * den_layer
        up_low = alb_dif * diffuse_low + alb_dir * direct_low
        return (direct_low, diffuse_low), (direct_low, diffuse_low, up_low)

    start_pair = (incoming, jnp.zeros_like(incoming))
    unused_pair, (direct_low, diffuse_low, up_low) = lax.scan(
        downward, start_pair, (trans_dir, trans_dif, refl_dif, scat_dir, below_dif, below_dir, inverse_den))
    net_low = direct_low + diffuse_low - up_low
    net_top = incoming - top_dir * incoming
    net_above = jnp.concatenate([net_top[None], net_low[:-1]], axis=0)
    heating = jnp.sum(net_above - net_low, axis=1) * (optical_depth.shape[0] / layer_mass[:, None])
    down_flux = jnp.sum(direct_low + diffuse_low, axis=1)
    return jnp.stack([heating, down_flux, jnp.sum(up_low, axis=1), jnp.sum(direct_low, axis=1)])


def periodic(field):
    return jnp.concatenate([field[:, :, -1:], field, field[:, :, :1]], axis=2)


def reference(prognostic, courant, daylit, cos_zenith, albedo, layer_mass, vapour_absorption, ozone_absorption, cloud_extinction, cloud_albedo, solar_weight):
    wall_mask = (lax.iota(jnp.int32, NY) > 0).astype(jnp.float32)

    def advect(level_parts):
        fields, winds = level_parts
        padded = periodic(fields)
        face_x = periodic(winds[:1])[:, :, 1:]
        face_y = winds[1:2] * wall_mask
        first_pass = donor(padded, face_x, face_y)
        padded_first = periodic(first_pass)
        speed_x, speed_y = corrective(padded_first, face_x, face_y)
        return donor(padded_first, speed_x, speed_y)

    level_fields = jnp.transpose(prognostic, (1, 0, 2, 3))[:, :, None]
    level_winds = jnp.transpose(courant, (1, 0, 2, 3))[:, :, None]
    advected = lax.map(advect, (level_fields, level_winds))
    advected = jnp.transpose(advected[:, :, 0], (1, 0, 2, 3))

    coarse = jnp.mean(prognostic[1:].reshape(3, LEV, NX // COARSEN, COARSEN, NY), axis=3).reshape(3, LEV, NCOARSE)
    optics = (layer_mass, vapour_absorption, ozone_absorption, cloud_extinction, cloud_albedo, solar_weight)

    def one_block(block_parts):
        profiles, cosine, ground_albedo, sunlit = block_parts
        return shortwave(profiles, cosine, ground_albedo, *optics) * sunlit.astype(jnp.float32)[None, None, :]

    block_profiles = jnp.transpose(coarse.reshape(3, LEV, N_TILE, CCOL), (2, 0, 1, 3))
    fluxes = lax.map(one_block, (block_profiles, cos_zenith.reshape(N_TILE, CCOL), albedo.reshape(N_TILE, CCOL), daylit.reshape(N_TILE, CCOL)))
    fluxes = jnp.transpose(fluxes, (1, 2, 0, 3)).reshape(4, LEV, NCOARSE)
    radiation_fine = jnp.broadcast_to(fluxes.reshape(4, LEV, NX // COARSEN, 1, NY), (4, LEV, NX // COARSEN, COARSEN, NY)).reshape(4, LEV, NX, NY)
    warmed = advected[0] + STEP_LENGTH * radiation_fine[0]
    dynamics_part = jnp.concatenate([warmed[None], advected[1:]], axis=0)
    return jnp.stack([dynamics_part, radiation_fine])
```

```python
import functools

import jax
import jax.numpy as jnp
from jax import lax
from jax.experimental import pallas as pl
from jax.experimental.pallas import tpu as pltpu
from jax.sharding import PartitionSpec as P

COARSEN = 4
DIFFUSIVITY = 1.66
STEP_LENGTH = 1.0
LOG2E = 1.4426950408889634
G_CHUNK = 8
LEVEL_BLOCK = 8
VMEM_LIMIT = 56 * 1024 * 1024


def pack_means(tile):
    sub = lax.broadcasted_iota(jnp.int32, (8, 128), 0) % 4
    packed = None
    for xh in range(2):
        for yh in range(2):
            part = tile[8 * xh : 8 * xh + 8, 128 * yh : 128 * yh + 128]
            part = part + pltpu.roll(part, 7, 0)
            part = part + pltpu.roll(part, 6, 0)
            k = 2 * xh + yh
            if k:
                part = pltpu.roll(part, k, 0)
            packed = part if packed is None else jnp.where(sub == k, part, packed)
    return packed * (1.0 / COARSEN)


def spread_part(packed, xh, yh):
    k = 2 * xh + yh
    low = jnp.broadcast_to(packed[k : k + 1], (8, 128))
    high = jnp.broadcast_to(packed[4 + k : 5 + k], (8, 128))
    return jnp.where(lax.broadcasted_iota(jnp.int32, (8, 128), 0) < 4, low, high)


def register_order(rows):
    return jnp.concatenate([rows[0:2], rows[4:6], rows[2:4], rows[6:8]], axis=0)


def radiation_kernel(
    mass_s, vap_s, oz_s, ext_s, alb_s, sol_s,
    lit_ref, cos_ref, ground_ref, prog_ref,
    out_ref, heat_ref,
    coarse, acc, k_tdir, k_a, k_b, k_ad, k_as,
):
    chunk = pl.program_id(0)
    levels = prog_ref.shape[1]

    @pl.when(chunk == 0)
    def _():
        def body(l, c):
            scale = mass_s[l]
            for f in range(3):
                coarse[f, l] = pack_means(prog_ref[f + 1, l]) * scale
            for f in range(4):
                acc[f, l] = jnp.zeros((8, 128), jnp.float32)
            return c

        lax.fori_loop(0, levels, body, 0, unroll=2)

    cosine = register_order(cos_ref[...])
    ground = register_order(ground_ref[...])
    dir_rate = -LOG2E / cosine
    dif_rate = -LOG2E * DIFFUSIVITY
    g0 = chunk * G_CHUNK
    oz = [oz_s[g0 + j] for j in range(G_CHUNK)]
    ext = [ext_s[g0 + j] for j in range(G_CHUNK)]
    half_alb = [0.5 * alb_s[g0 + j] for j in range(G_CHUNK)]

    def upward(i, carry):
        l = levels - 1 - i
        alb_dif, alb_dir = carry
        vapour, cloud, ozone = coarse[0, l], coarse[1, l], coarse[2, l]
        new_dif, new_dir = [], []
        for j in range(G_CHUNK):
            cloud_depth = cloud * ext[j]
            depth = (vapour * vap_s[l, g0 + j] + ozone * oz[j]) + cloud_depth
            half_w = (cloud_depth * half_alb[j]) / depth
            t_dir = jnp.exp2(depth * dir_rate)
            t_dif = jnp.exp2(depth * dif_rate)
            t_sq = t_dif * t_dif
            r_dif = half_w * (1.0 - t_sq)
            s_dir = half_w * (1.0 - t_dir)
            den = 1.0 / (1.0 - r_dif * alb_dif[j])
            through = alb_dir[j] * t_dir
            down = (s_dir + r_dif * through) * den
            k_tdir[l, j] = t_dir
            k_a[l, j] = t_dif * den
            k_b[l, j] = down
            k_ad[l, j] = alb_dif[j]
            k_as[l, j] = alb_dir[j]
            new_dir.append(s_dir + t_dif * (alb_dif[j] * down + through))
            new_dif.append(r_dif + t_sq * alb_dif[j] * den)
        return tuple(new_dif), tuple(new_dir)

    start = (ground,) * G_CHUNK
    _, top_dir = lax.fori_loop(0, levels, upward, (start, start))

    direct0 = tuple(cosine * sol_s[g0 + j] for j in range(G_CHUNK))
    net0 = tuple(d - t * d for d, t in zip(direct0, top_dir))
    diffuse0 = tuple(jnp.zeros((8, 128), jnp.float32) for _ in range(G_CHUNK))

    def downward(l, carry):
        direct, diffuse, net = carry
        n_direct, n_diffuse, n_net = [], [], []
        sums = None
        for j in range(G_CHUNK):
            s_low = direct[j] * k_tdir[l, j]
            d_low = diffuse[j] * k_a[l, j] + direct[j] * k_b[l, j]
            up = k_ad[l, j] * d_low + k_as[l, j] * s_low
            total = s_low + d_low
            low_net = total - up
            terms = (net[j] - low_net, total, up, s_low)
            sums = terms if sums is None else tuple(a + b for a, b in zip(sums, terms))
            n_direct.append(s_low)
            n_diffuse.append(d_low)
            n_net.append(low_net)
        for f in range(4):
            acc[f, l] += sums[f]
        return tuple(n_direct), tuple(n_diffuse), tuple(n_net)

    lax.fori_loop(0, levels, downward, (direct0, diffuse0, net0))

    @pl.when(chunk == pl.num_programs(0) - 1)
    def _():
        lit = register_order(lit_ref[...]).astype(jnp.float32)

        def body(l, c):
            scale = jnp.full((8, 128), float(levels)) / jnp.full((8, 128), mass_s[l])
            for f in range(4):
                value = acc[f, l] * lit
                if f == 0:
                    value = value * scale
                    heat_ref[l] = value
                for xh in range(2):
                    for yh in range(2):
                        out_ref[f, l, 8 * xh : 8 * xh + 8, 128 * yh : 128 * yh + 128] = (
                            spread_part(value, xh, yh)
                        )
            return c

        lax.fori_loop(0, levels, body, 0)


def radiation(prognostic, daylit, cos_zenith, albedo, optics):
    fields, levels, cells_x, cells_y = prognostic.shape
    g_points = optics[1].shape[1]
    smem = pl.BlockSpec(memory_space=pltpu.SMEM)
    vec = pl.BlockSpec((8, 128), lambda c: (0, 0))
    whole = pl.BlockSpec(prognostic.shape, lambda c: (0, 0, 0, 0), pipeline_mode=pl.Buffered(1))
    kept = pltpu.VMEM((levels, G_CHUNK, 8, 128), jnp.float32)
    return pl.pallas_call(
        radiation_kernel,
        grid=(g_points // G_CHUNK,),
        in_specs=[smem] * 6 + [vec] * 3 + [whole],
        out_specs=[
            pl.BlockSpec(prognostic.shape, lambda c: (0, 0, 0, 0)),
            pl.BlockSpec((levels, 8, 128), lambda c: (0, 0, 0)),
        ],
        out_shape=[
            jax.ShapeDtypeStruct(prognostic.shape, jnp.float32),
            jax.ShapeDtypeStruct((levels, 8, 128), jnp.float32),
        ],
        scratch_shapes=[
            pltpu.VMEM((3, levels, 8, 128), jnp.float32),
            pltpu.VMEM((4, levels, 8, 128), jnp.float32),
            kept, kept, kept, kept, kept,
        ],
        compiler_params=pltpu.CompilerParams(vmem_limit_bytes=VMEM_LIMIT),
        name="radiation",
    )(
        *optics,
        daylit.reshape(8, 128), cos_zenith.reshape(8, 128), albedo.reshape(8, 128),
        prognostic,
    )


def dynamics_kernel(
    prog_ref, cour_ref, left_ref, right_ref, out_ref, first, row_m1, row_15, row_16, flux_16
):
    fields, block, cells_x, cells_y = prog_ref.shape
    shape = (cells_x, cells_y)
    row = lax.broadcasted_iota(jnp.int32, shape, 0)
    wall = (lax.broadcasted_iota(jnp.int32, shape, 1) > 0).astype(jnp.float32)
    is_first, is_last = row == 0, row == cells_x - 1
    last = cells_x - 1

    def before_x(value, halo):
        return jnp.where(is_first, halo, pltpu.roll(value, 1, 0))

    def after_x(value, halo):
        return jnp.where(is_last, halo, pltpu.roll(value, cells_x - 1, 0))

    def spread_y(flux):
        return pltpu.roll(flux, cells_y - 1, 1) - flux

    def pass_one(l, c):
        u = cour_ref[0, l]
        v = cour_ref[1, l] * wall
        up, um = jnp.maximum(u, 0.0), jnp.minimum(u, 0.0)
        vp, vm = jnp.maximum(v, 0.0), jnp.minimum(v, 0.0)
        u16 = right_ref[2 * fields, pl.ds(l, 1), :]
        up16, um16 = jnp.maximum(u16, 0.0), jnp.minimum(u16, 0.0)
        for f in range(fields):
            p = prog_ref[f, l]
            flux = up * before_x(p, left_ref[f, pl.ds(l, 1), :]) + um * p
            end = up16 * p[last:] + um16 * right_ref[f, pl.ds(l, 1), :]
            flux_y = vp * pltpu.roll(p, 1, 1) + vm * p
            result = p - (after_x(flux, end) - flux) - spread_y(flux_y)
            first[f, l] = result
            row_15[f, pl.ds(l, 1), :] = result[last:]
            row_m1[f, pl.ds(l, 1), :] = left_ref[fields + f, pl.ds(l, 1), :] - flux[:1]
            row_16[f, pl.ds(l, 1), :] = right_ref[fields + f, pl.ds(l, 1), :] + end
        return c

    lax.fori_loop(0, block, pass_one, 0)

    u16 = right_ref[2 * fields]
    gain16 = jnp.abs(u16) - u16 * u16
    for f in range(fields):
        lo, hi = row_15[f], row_16[f]
        speed = gain16 * (hi - lo) / (hi + lo)
        flux_16[f] = jnp.maximum(speed, 0.0) * lo + jnp.minimum(speed, 0.0) * hi

    def pass_two(l, c):
        u = cour_ref[0, l]
        v = cour_ref[1, l] * wall
        gain_x = jnp.abs(u) - u * u
        gain_y = jnp.abs(v) - v * v
        for f in range(fields):
            p = first[f, l]
            lo = before_x(p, row_m1[f, pl.ds(l, 1), :])
            speed = gain_x * (p - lo) / (p + lo)
            flux = jnp.maximum(speed, 0.0) * lo + jnp.minimum(speed, 0.0) * p
            lo = pltpu.roll(p, 1, 1)
            speed = gain_y * (p - lo) / (p + lo)
            flux_y = jnp.maximum(speed, 0.0) * lo + jnp.minimum(speed, 0.0) * p
            end = flux_16[f, pl.ds(l, 1), :]
            out_ref[f, l] = p - (after_x(flux, end) - flux) - spread_y(flux_y)
        return c

    lax.fori_loop(0, block, pass_two, 0)


def advance(prognostic, courant, left, right):
    fields, levels, cells_x, cells_y = prognostic.shape
    block = LEVEL_BLOCK
    rows = pltpu.VMEM((fields, block, cells_y), jnp.float32)
    return pl.pallas_call(
        dynamics_kernel,
        grid=(levels // block,),
        in_specs=[
            pl.BlockSpec((fields, block, cells_x, cells_y), lambda i: (0, i, 0, 0)),
            pl.BlockSpec((2, block, cells_x, cells_y), lambda i: (0, i, 0, 0)),
            pl.BlockSpec((left.shape[0], block, cells_y), lambda i: (0, i, 0)),
            pl.BlockSpec((right.shape[0], block, cells_y), lambda i: (0, i, 0)),
        ],
        out_specs=pl.BlockSpec((fields, block, cells_x, cells_y), lambda i: (0, i, 0, 0)),
        out_shape=jax.ShapeDtypeStruct(prognostic.shape, jnp.float32),
        scratch_shapes=[
            pltpu.VMEM((fields, block, cells_x, cells_y), jnp.float32), rows, rows, rows, rows,
        ],
        compiler_params=pltpu.CompilerParams(vmem_limit_bytes=VMEM_LIMIT),
        name="advance",
    )(prognostic, courant, left, right)


def warm_kernel(field_ref, heat_ref, out_ref):
    def body(l, c):
        packed = heat_ref[l] * STEP_LENGTH
        for xh in range(2):
            for yh in range(2):
                part = (0, l, slice(8 * xh, 8 * xh + 8), slice(128 * yh, 128 * yh + 128))
                out_ref[part] = field_ref[part] + spread_part(packed, xh, yh)
        return c

    lax.fori_loop(0, heat_ref.shape[0], body, 0, unroll=4)


def warm(fields, heat):
    _, levels, cells_x, cells_y = fields.shape
    block = 16
    spec = pl.BlockSpec((1, block, cells_x, cells_y), lambda i: (0, i, 0, 0))
    return pl.pallas_call(
        warm_kernel,
        grid=(levels // block,),
        in_specs=[spec, pl.BlockSpec((block, 8, 128), lambda i: (i, 0, 0))],
        out_specs=spec,
        out_shape=jax.ShapeDtypeStruct(fields.shape, jnp.float32),
        input_output_aliases={0: 0},
        name="warm",
    )(fields, heat)


def upwind(low, high, face):
    return jnp.maximum(face, 0.0) * low + jnp.minimum(face, 0.0) * high


def across_y(value, face):
    flux = upwind(jnp.roll(value, 1, axis=-1), value, face)
    return jnp.roll(flux, -1, axis=-1) - flux


def edge_rows(prognostic, courant):
    u, v = courant
    wall = (lax.iota(jnp.int32, v.shape[-1]) > 0).astype(jnp.float32)
    end, inner = prognostic[:, :, -1], prognostic[:, :, -2]
    partial = end + upwind(inner, end, u[:, -1]) - across_y(end, v[:, -1] * wall)
    to_right = jnp.concatenate([end, partial], axis=0)
    start, inner = prognostic[:, :, 0], prognostic[:, :, 1]
    partial = start - upwind(start, inner, u[:, 1]) - across_y(start, v[:, 0] * wall)
    to_left = jnp.concatenate([start, partial, u[None, :, 0]], axis=0)
    return to_right, to_left


def per_device(prognostic, courant, daylit, cos_zenith, albedo, *optics):
    dynamics = lax.axis_index("grp") == 0
    tiles = lax.axis_size("tile")
    to_right, to_left = edge_rows(prognostic, courant)
    left = lax.ppermute(to_right, ("grp", "tile"), [(i, (i + 1) % tiles) for i in range(tiles)])
    right = lax.ppermute(to_left, ("grp", "tile"), [((i + 1) % tiles, i) for i in range(tiles)])
    levels = prognostic.shape[1]

    def run_dynamics(left, right):
        return advance(prognostic, courant, left, right), jnp.zeros((levels, 8, 128), jnp.float32)

    def run_radiation(left, right):
        out, heat = radiation(prognostic, daylit, cos_zenith, albedo, optics)
        return out, heat

    fields, heat = lax.cond(dynamics, run_dynamics, run_radiation, left, right)
    heat = lax.ppermute(heat, "grp", [(1, 0)])
    return warm(fields, heat)[None]


def solution(mesh):
    column = P("tile")
    plane = P(None, None, "tile", None)
    return jax.shard_map(
        per_device,
        mesh=mesh,
        in_specs=(plane, plane, column, column, column) + (P(),) * 6,
        out_specs=P("grp", None, None, "tile", None),
        check_vma=False,
    )
```

```python
import functools

import jax
import jax.numpy as jnp
from jax import lax
from jax.experimental import pallas as pl
from jax.experimental.pallas import tpu as pltpu
from jax.sharding import PartitionSpec as P

COARSEN = 4
DIFFUSIVITY = 1.66
STEP_LENGTH = 1.0
LOG2E = 1.4426950408889634
G_CHUNK = 8
LEVEL_BLOCK = 8
VMEM_LIMIT = 56 * 1024 * 1024


def pack_means(tile):
    sub = lax.broadcasted_iota(jnp.int32, (8, 128), 0) % 4
    packed = None
    for xh in range(2):
        for yh in range(2):
            part = tile[8 * xh : 8 * xh + 8, 128 * yh : 128 * yh + 128]
            part = part + pltpu.roll(part, 7, 0)
            part = part + pltpu.roll(part, 6, 0)
            k = 2 * xh + yh
            if k:
                part = pltpu.roll(part, k, 0)
            packed = part if packed is None else jnp.where(sub == k, part, packed)
    return packed * (1.0 / COARSEN)


def spread_part(packed, xh, yh):
    k = 2 * xh + yh
    low = jnp.broadcast_to(packed[k : k + 1], (8, 128))
    high = jnp.broadcast_to(packed[4 + k : 5 + k], (8, 128))
    return jnp.where(lax.broadcasted_iota(jnp.int32, (8, 128), 0) < 4, low, high)


def register_order(rows):
    return jnp.concatenate([rows[0:2], rows[4:6], rows[2:4], rows[6:8]], axis=0)


def radiation_kernel(
    mass_s, vap_s, oz_s, ext_s, alb_s, sol_s,
    lit_ref, cos_ref, ground_ref, vapour_ref, cloud_ref, ozone_ref,
    unused_ref, heat_ref, acc,
    coarse, k_tdir, k_a, k_b, k_ad, k_as,
):
    chunk = pl.program_id(0)
    levels = acc.shape[1]

    @pl.when(chunk == 0)
    def _():
        def body(l, c):
            scale = mass_s[l]
            for f, ref in enumerate((vapour_ref, cloud_ref, ozone_ref)):
                coarse[f, l] = pack_means(ref[0, l]) * scale
            for f in range(4):
                acc[f, l] = jnp.zeros((8, 128), jnp.float32)
            return c

        lax.fori_loop(0, levels, body, 0, unroll=2)

    cosine = register_order(cos_ref[...])
    ground = register_order(ground_ref[...])
    dir_rate = -LOG2E / cosine
    dif_rate = -LOG2E * DIFFUSIVITY
    g0 = chunk * G_CHUNK
    oz = [oz_s[g0 + j] for j in range(G_CHUNK)]
    ext = [ext_s[g0 + j] for j in range(G_CHUNK)]
    half_alb = [0.5 * alb_s[g0 + j] for j in range(G_CHUNK)]

    def upward(i, carry):
        l = levels - 1 - i
        alb_dif, alb_dir = carry
        vapour, cloud, ozone = coarse[0, l], coarse[1, l], coarse[2, l]
        new_dif, new_dir = [], []
        for j in range(G_CHUNK):
            cloud_depth = cloud * ext[j]
            depth = (vapour * vap_s[l, g0 + j] + ozone * oz[j]) + cloud_depth
            half_w = (cloud_depth * half_alb[j]) * inverse(depth)
            t_dir = jnp.exp2(depth * dir_rate)
            t_dif = jnp.exp2(depth * dif_rate)
            t_sq = t_dif * t_dif
            r_dif = half_w * (1.0 - t_sq)
            s_dir = half_w * (1.0 - t_dir)
            den = inverse(1.0 - r_dif * alb_dif[j])
            through = alb_dir[j] * t_dir
            down = (s_dir + r_dif * through) * den
            k_tdir[l, j] = t_dir
            k_a[l, j] = t_dif * den
            k_b[l, j] = down
            k_ad[l, j] = alb_dif[j]
            k_as[l, j] = alb_dir[j]
            new_dir.append(s_dir + t_dif * (alb_dif[j] * down + through))
            new_dif.append(r_dif + t_sq * alb_dif[j] * den)
        return tuple(new_dif), tuple(new_dir)

    start = (ground,) * G_CHUNK
    _, top_dir = lax.fori_loop(0, levels, upward, (start, start))

    direct0 = tuple(cosine * sol_s[g0 + j] for j in range(G_CHUNK))
    net0 = tuple(d - t * d for d, t in zip(direct0, top_dir))
    diffuse0 = tuple(jnp.zeros((8, 128), jnp.float32) for _ in range(G_CHUNK))

    def downward(l, carry):
        direct, diffuse, net = carry
        n_direct, n_diffuse, n_net = [], [], []
        sums = None
        for j in range(G_CHUNK):
            s_low = direct[j] * k_tdir[l, j]
            d_low = diffuse[j] * k_a[l, j] + direct[j] * k_b[l, j]
            up = k_ad[l, j] * d_low + k_as[l, j] * s_low
            total = s_low + d_low
            low_net = total - up
            terms = (net[j] - low_net, total, up, s_low)
            sums = terms if sums is None else tuple(a + b for a, b in zip(sums, terms))
            n_direct.append(s_low)
            n_diffuse.append(d_low)
            n_net.append(low_net)
        for f in range(4):
            acc[f, l] += sums[f]
        return tuple(n_direct), tuple(n_diffuse), tuple(n_net)

    lax.fori_loop(0, levels, downward, (direct0, diffuse0, net0))

    @pl.when(chunk == pl.num_programs(0) - 1)
    def _():
        lit = register_order(lit_ref[...]).astype(jnp.float32)

        def body(l, c):
            heat_ref[l] = acc[0, l] * lit * (float(levels) / jnp.full((8, 128), mass_s[l]))
            return c

        lax.fori_loop(0, levels, body, 0, unroll=4)


def radiation(prognostic, daylit, cos_zenith, albedo, optics):
    fields, levels, cells_x, cells_y = prognostic.shape
    g_points = optics[1].shape[1]
    smem = pl.BlockSpec(memory_space=pltpu.SMEM)
    vec = pl.BlockSpec((8, 128), lambda c: (0, 0))
    field_specs = [
        pl.BlockSpec(
            (1, levels, cells_x, cells_y), lambda c, f=f: (f, 0, 0, 0), pipeline_mode=pl.Buffered(1)
        )
        for f in range(1, 4)
    ]
    kept = pltpu.VMEM((levels, G_CHUNK, 8, 128), jnp.float32)
    return pl.pallas_call(
        radiation_kernel,
        grid=(g_points // G_CHUNK,),
        in_specs=[smem] * 6 + [vec] * 3 + field_specs,
        out_specs=[
            pl.BlockSpec(memory_space=pl.ANY),
            pl.BlockSpec((levels, 8, 128), lambda c: (0, 0, 0)),
            pl.BlockSpec((4, levels, 8, 128), lambda c: (0, 0, 0, 0)),
        ],
        out_shape=[
            jax.ShapeDtypeStruct(prognostic.shape, jnp.float32),
            jax.ShapeDtypeStruct((levels, 8, 128), jnp.float32),
            jax.ShapeDtypeStruct((4, levels, 8, 128), jnp.float32),
        ],
        scratch_shapes=[pltpu.VMEM((3, levels, 8, 128), jnp.float32), kept, kept, kept, kept, kept],
        compiler_params=pltpu.CompilerParams(vmem_limit_bytes=VMEM_LIMIT),
        name="radiation",
    )(
        *optics,
        daylit.reshape(8, 128), cos_zenith.reshape(8, 128), albedo.reshape(8, 128),
        prognostic, prognostic, prognostic,
    )


def expand_kernel(lit_ref, heat_ref, acc_ref, out_ref):
    lit = register_order(lit_ref[...]).astype(jnp.float32)

    def body(l, c):
        for f in range(4):
            value = heat_ref[l] if f == 0 else acc_ref[f, l] * lit
            for xh in range(2):
                for yh in range(2):
                    out_ref[f, l, 8 * xh : 8 * xh + 8, 128 * yh : 128 * yh + 128] = spread_part(
                        value, xh, yh
                    )
        return c

    lax.fori_loop(0, heat_ref.shape[0], body, 0, unroll=2)


def expand(daylit, heat, fluxes, shape):
    fields, levels, cells_x, cells_y = shape
    block = LEVEL_BLOCK
    return pl.pallas_call(
        expand_kernel,
        grid=(levels // block,),
        in_specs=[
            pl.BlockSpec((8, 128), lambda i: (0, 0)),
            pl.BlockSpec((block, 8, 128), lambda i: (i, 0, 0)),
            pl.BlockSpec((4, block, 8, 128), lambda i: (0, i, 0, 0)),
        ],
        out_specs=pl.BlockSpec((fields, block, cells_x, cells_y), lambda i: (0, i, 0, 0)),
        out_shape=jax.ShapeDtypeStruct(shape, jnp.float32),
        name="expand",
    )(daylit.reshape(8, 128), heat, fluxes)


def inverse(value):
    return pl.reciprocal(value, approx=False)


def wall_mask(shape):
    return (lax.broadcasted_iota(jnp.int32, shape, len(shape) - 1) > 0).astype(jnp.float32)


def upwind(low, high, face):
    return jnp.maximum(face, 0.0) * low + jnp.minimum(face, 0.0) * high


def across_y(value, face):
    flux = upwind(pltpu.roll(value, 1, 1), value, face)
    return pltpu.roll(flux, value.shape[1] - 1, 1) - flux


def edges_kernel(prog_ref, cour_ref, right_ref, left_ref, rows):
    fields, block, cells_x, cells_y = prog_ref.shape
    last = cells_x - 1
    picks = [(prog_ref, f, x) for x in (last, last - 1, 0, 1) for f in range(fields)]
    picks += [(cour_ref, 0, last), (cour_ref, 0, 1), (cour_ref, 0, 0), (cour_ref, 1, last), (cour_ref, 1, 0)]
    for l in range(block):
        for k, (ref, f, x) in enumerate(picks):
            rows[k, l : l + 1, :] = ref[f, l, x : x + 1, :]
    base = 4 * fields
    u_last, u_one, u_zero = rows[base], rows[base + 1], rows[base + 2]
    wall = wall_mask((block, cells_y))
    v_last, v_zero = rows[base + 3] * wall, rows[base + 4] * wall
    for f in range(fields):
        end, inner = rows[f], rows[fields + f]
        right_ref[f] = end
        right_ref[fields + f] = end + upwind(inner, end, u_last) - across_y(end, v_last)
        start, inner = rows[2 * fields + f], rows[3 * fields + f]
        left_ref[f] = start
        left_ref[fields + f] = start - upwind(start, inner, u_one) - across_y(start, v_zero)
    left_ref[2 * fields] = u_zero


def edges(prognostic, courant):
    fields, levels, cells_x, cells_y = prognostic.shape
    block = LEVEL_BLOCK
    return pl.pallas_call(
        edges_kernel,
        grid=(levels // block,),
        in_specs=[
            pl.BlockSpec((fields, block, cells_x, cells_y), lambda i: (0, i, 0, 0)),
            pl.BlockSpec((2, block, cells_x, cells_y), lambda i: (0, i, 0, 0)),
        ],
        out_specs=[
            pl.BlockSpec((2 * fields, block, cells_y), lambda i: (0, i, 0)),
            pl.BlockSpec((2 * fields + 1, block, cells_y), lambda i: (0, i, 0)),
        ],
        out_shape=[
            jax.ShapeDtypeStruct((2 * fields, levels, cells_y), jnp.float32),
            jax.ShapeDtypeStruct((2 * fields + 1, levels, cells_y), jnp.float32),
        ],
        scratch_shapes=[pltpu.VMEM((4 * fields + 5, block, cells_y), jnp.float32)],
        name="edges",
    )(prognostic, courant)


def no_edges(prognostic):
    fields, levels, _, cells_y = prognostic.shape
    return pl.pallas_call(
        lambda right_ref, left_ref: None,
        out_specs=[pl.BlockSpec(memory_space=pl.ANY)] * 2,
        out_shape=[
            jax.ShapeDtypeStruct((2 * fields, levels, cells_y), jnp.float32),
            jax.ShapeDtypeStruct((2 * fields + 1, levels, cells_y), jnp.float32),
        ],
        name="no_edges",
    )()


def pass_one_kernel(prog_ref, cour_ref, first_ref, heat_ref, acc_ref):
    fields, block, cells_x, cells_y = prog_ref.shape
    shape = (cells_x, cells_y)
    wall = wall_mask(shape)
    inside = (lax.broadcasted_iota(jnp.int32, shape, 0) > 0).astype(jnp.float32)

    def body(l, c):
        u = cour_ref[0, l] * inside
        v = cour_ref[1, l] * wall
        up, um = jnp.maximum(u, 0.0), jnp.minimum(u, 0.0)
        vp, vm = jnp.maximum(v, 0.0), jnp.minimum(v, 0.0)
        for f in range(fields):
            p = prog_ref[f, l]
            flux = up * pltpu.roll(p, 1, 0) + um * p
            flux_y = vp * pltpu.roll(p, 1, 1) + vm * p
            first_ref[f, l] = (
                p
                - (pltpu.roll(flux, cells_x - 1, 0) - flux)
                - (pltpu.roll(flux_y, cells_y - 1, 1) - flux_y)
            )
        return c

    lax.fori_loop(0, block, body, 0)


def pass_one(prognostic, courant):
    fields, levels, cells_x, cells_y = prognostic.shape
    block = LEVEL_BLOCK
    plane = pl.BlockSpec((fields, block, cells_x, cells_y), lambda i: (0, i, 0, 0))
    return pl.pallas_call(
        pass_one_kernel,
        grid=(levels // block,),
        in_specs=[plane, pl.BlockSpec((2, block, cells_x, cells_y), lambda i: (0, i, 0, 0))],
        out_specs=[plane, pl.BlockSpec(memory_space=pl.ANY), pl.BlockSpec(memory_space=pl.ANY)],
        out_shape=[
            jax.ShapeDtypeStruct(prognostic.shape, jnp.float32),
            jax.ShapeDtypeStruct((levels, 8, 128), jnp.float32),
            jax.ShapeDtypeStruct((4, levels, 8, 128), jnp.float32),
        ],
        name="pass_one",
    )(prognostic, courant)


def pass_two_kernel(
    first_ref, edge_ref, cour_ref, left_ref, right_ref, out_ref, rows, row_m1, row_0, row_15, flux_16
):
    fields, block, cells_x, cells_y = first_ref.shape
    shape = (cells_x, cells_y)
    last = cells_x - 1
    row = lax.broadcasted_iota(jnp.int32, shape, 0)
    wall = wall_mask(shape)
    is_first, is_last = row == 0, row == last

    for l in range(block):
        rows[2 * fields, l : l + 1, :] = cour_ref[0, l, :1, :]
        for f in range(fields):
            rows[f, l : l + 1, :] = edge_ref[f, l, :1, :]
            rows[fields + f, l : l + 1, :] = edge_ref[f, l, last:, :]
            row_0[f, l : l + 1, :] = first_ref[f, l, :1, :]
            row_15[f, l : l + 1, :] = first_ref[f, l, last:, :]
    u0, u16 = rows[2 * fields], right_ref[2 * fields]
    gain = jnp.abs(u16) - u16 * u16
    for f in range(fields):
        begin = upwind(left_ref[f], rows[f], u0)
        end = upwind(rows[fields + f], right_ref[f], u16)
        row_m1[f] = left_ref[fields + f] - begin
        row_0[f] = row_0[f] + begin
        lo = row_15[f] - end
        hi = right_ref[fields + f] + end
        row_15[f] = lo
        speed = gain * (hi - lo) * inverse(hi + lo)
        flux_16[f] = upwind(lo, hi, speed)

    def body(l, c):
        u = cour_ref[0, l]
        v = cour_ref[1, l] * wall
        gain_x = jnp.abs(u) - u * u
        gain_y = jnp.abs(v) - v * v
        one = pl.ds(l, 1)
        for f in range(fields):
            p = first_ref[f, l]
            p = jnp.where(is_first, row_0[f, one, :], jnp.where(is_last, row_15[f, one, :], p))
            lo = jnp.where(is_first, row_m1[f, one, :], pltpu.roll(p, 1, 0))
            flux = upwind(lo, p, gain_x * (p - lo) * inverse(p + lo))
            lo = pltpu.roll(p, 1, 1)
            flux_y = upwind(lo, p, gain_y * (p - lo) * inverse(p + lo))
            beyond = jnp.where(is_last, flux_16[f, one, :], pltpu.roll(flux, last, 0))
            out_ref[f, l] = p - (beyond - flux) - (pltpu.roll(flux_y, cells_y - 1, 1) - flux_y)
        return c

    lax.fori_loop(0, block, body, 0)


def pass_two(first, prognostic, courant, left, right):
    fields, levels, cells_x, cells_y = first.shape
    block = LEVEL_BLOCK
    plane = pl.BlockSpec((fields, block, cells_x, cells_y), lambda i: (0, i, 0, 0))
    rows = pltpu.VMEM((fields, block, cells_y), jnp.float32)
    return pl.pallas_call(
        pass_two_kernel,
        grid=(levels // block,),
        in_specs=[
            plane,
            plane,
            pl.BlockSpec((2, block, cells_x, cells_y), lambda i: (0, i, 0, 0)),
            pl.BlockSpec((left.shape[0], block, cells_y), lambda i: (0, i, 0)),
            pl.BlockSpec((right.shape[0], block, cells_y), lambda i: (0, i, 0)),
        ],
        out_specs=plane,
        out_shape=jax.ShapeDtypeStruct(first.shape, jnp.float32),
        scratch_shapes=[
            pltpu.VMEM((2 * fields + 1, block, cells_y), jnp.float32), rows, rows, rows, rows,
        ],
        name="pass_two",
    )(first, prognostic, courant, left, right)


def warm_kernel(field_ref, heat_ref, out_ref):
    block = field_ref.shape[1]
    start = pl.program_id(0) * block

    def body(l, c):
        packed = heat_ref[start + l] * STEP_LENGTH
        for xh in range(2):
            for yh in range(2):
                part = (0, l, slice(8 * xh, 8 * xh + 8), slice(128 * yh, 128 * yh + 128))
                out_ref[part] = field_ref[part] + spread_part(packed, xh, yh)
        return c

    lax.fori_loop(0, block, body, 0, unroll=4)


def warm(fields, heat):
    _, levels, cells_x, cells_y = fields.shape
    block = 16
    spec = pl.BlockSpec((1, block, cells_x, cells_y), lambda i: (0, i, 0, 0))
    return pl.pallas_call(
        warm_kernel,
        grid=(levels // block,),
        in_specs=[spec, pl.BlockSpec(memory_space=pltpu.VMEM)],
        out_specs=spec,
        out_shape=jax.ShapeDtypeStruct(fields.shape, jnp.float32),
        input_output_aliases={0: 0},
        name="warm",
    )(fields, heat)


def per_device(prognostic, courant, daylit, cos_zenith, albedo, *optics):
    dynamics = lax.axis_index("grp") == 0
    tiles = lax.axis_size("tile")
    to_right, to_left = lax.cond(
        dynamics, lambda: edges(prognostic, courant), lambda: no_edges(prognostic)
    )
    left = lax.ppermute(to_right, ("grp", "tile"), [(i, (i + 1) % tiles) for i in range(tiles)])
    right = lax.ppermute(to_left, ("grp", "tile"), [((i + 1) % tiles, i) for i in range(tiles)])
    first, heat, fluxes = lax.cond(
        dynamics,
        lambda: pass_one(prognostic, courant),
        lambda: radiation(prognostic, daylit, cos_zenith, albedo, optics),
    )
    heat_in = lax.ppermute(heat, "grp", [(1, 0)])
    fields = lax.cond(
        dynamics,
        lambda left, right: pass_two(first, prognostic, courant, left, right),
        lambda left, right: expand(daylit, heat, fluxes, prognostic.shape),
        left, right,
    )
    return warm(fields, heat_in)[None]


def solution(mesh):
    column = P("tile")
    plane = P(None, None, "tile", None)
    return jax.shard_map(
        per_device,
        mesh=mesh,
        in_specs=(plane, plane, column, column, column) + (P(),) * 6,
        out_specs=P("grp", None, None, "tile", None),
        check_vma=False,
    )
```

```python
import functools

import jax
import jax.numpy as jnp
from jax import lax
from jax.experimental import pallas as pl
from jax.experimental.pallas import tpu as pltpu
from jax.sharding import PartitionSpec as P

COARSEN = 4
DIFFUSIVITY = 1.66
STEP_LENGTH = 1.0
LOG2E = 1.4426950408889634
G_CHUNK = 8
UP_UNROLL = 2
DOWN_UNROLL = 1
EDGE_BLOCK = 16
ONE_BLOCK = 16
ONE_UNROLL = 4
TWO_BLOCK = 16
TWO_UNROLL = 4
EXPAND_BLOCK = 16
WARM_BLOCK = 16
SOLVE_VMEM = 24 * 1024 * 1024
SMALL_VMEM = 16 * 1024 * 1024


def pack_means(tile):
    sub = lax.broadcasted_iota(jnp.int32, (8, 128), 0) % 4
    packed = None
    for xh in range(2):
        for yh in range(2):
            part = tile[8 * xh : 8 * xh + 8, 128 * yh : 128 * yh + 128]
            part = part + pltpu.roll(part, 7, 0)
            part = part + pltpu.roll(part, 6, 0)
            k = 2 * xh + yh
            if k:
                part = pltpu.roll(part, k, 0)
            packed = part if packed is None else jnp.where(sub == k, part, packed)
    return packed * (1.0 / COARSEN)


def spread_part(packed, xh, yh):
    k = 2 * xh + yh
    low = jnp.broadcast_to(packed[k : k + 1], (8, 128))
    high = jnp.broadcast_to(packed[4 + k : 5 + k], (8, 128))
    return jnp.where(lax.broadcasted_iota(jnp.int32, (8, 128), 0) < 4, low, high)


def register_order(rows):
    return jnp.concatenate([rows[0:2], rows[4:6], rows[2:4], rows[6:8]], axis=0)


def radiation_kernel(
    mass_s, vap_s, oz_s, ext_s, alb_s, sol_s,
    lit_ref, cos_ref, ground_ref, vapour_ref, cloud_ref, ozone_ref,
    unused_ref, heat_ref, acc,
    coarse, k_tdir, k_a, k_b, k_ad, k_as,
):
    chunk = pl.program_id(0)
    levels = acc.shape[1]

    @pl.when(chunk == 0)
    def _():
        def body(l, c):
            scale = mass_s[l]
            for f, ref in enumerate((vapour_ref, cloud_ref, ozone_ref)):
                coarse[f, l] = pack_means(ref[0, l]) * scale
            for f in range(4):
                acc[f, l] = jnp.zeros((8, 128), jnp.float32)
            return c

        lax.fori_loop(0, levels, body, 0, unroll=2)

    cosine = register_order(cos_ref[...])
    ground = register_order(ground_ref[...])
    dir_rate = -LOG2E / cosine
    dif_rate = -LOG2E * DIFFUSIVITY
    g0 = chunk * G_CHUNK
    oz = [oz_s[g0 + j] for j in range(G_CHUNK)]
    ext = [ext_s[g0 + j] for j in range(G_CHUNK)]
    half_alb = [0.5 * alb_s[g0 + j] for j in range(G_CHUNK)]

    def upward(i, carry):
        l = levels - 1 - i
        alb_dif, alb_dir = carry
        vapour, cloud, ozone = coarse[0, l], coarse[1, l], coarse[2, l]
        new_dif, new_dir = [], []
        for j in range(G_CHUNK):
            cloud_depth = cloud * ext[j]
            depth = (vapour * vap_s[l, g0 + j] + ozone * oz[j]) + cloud_depth
            half_w = (cloud_depth * half_alb[j]) * inverse(depth)
            t_dir = jnp.exp2(depth * dir_rate)
            t_dif = jnp.exp2(depth * dif_rate)
            t_sq = t_dif * t_dif
            r_dif = half_w * (1.0 - t_sq)
            s_dir = half_w * (1.0 - t_dir)
            den = inverse(1.0 - r_dif * alb_dif[j])
            through = alb_dir[j] * t_dir
            down = (s_dir + r_dif * through) * den
            k_tdir[l, j] = t_dir
            k_a[l, j] = t_dif * den
            k_b[l, j] = down
            k_ad[l, j] = alb_dif[j]
            k_as[l, j] = alb_dir[j]
            new_dir.append(s_dir + t_dif * (alb_dif[j] * down + through))
            new_dif.append(r_dif + t_sq * alb_dif[j] * den)
        return tuple(new_dif), tuple(new_dir)

    start = (ground,) * G_CHUNK
    _, top_dir = lax.fori_loop(0, levels, upward, (start, start), unroll=UP_UNROLL)

    direct0 = tuple(cosine * sol_s[g0 + j] for j in range(G_CHUNK))
    net0 = tuple(d - t * d for d, t in zip(direct0, top_dir))
    diffuse0 = tuple(jnp.zeros((8, 128), jnp.float32) for _ in range(G_CHUNK))

    def downward(l, carry):
        direct, diffuse, net = carry
        n_direct, n_diffuse, n_net = [], [], []
        sums = None
        for j in range(G_CHUNK):
            s_low = direct[j] * k_tdir[l, j]
            d_low = diffuse[j] * k_a[l, j] + direct[j] * k_b[l, j]
            up = k_ad[l, j] * d_low + k_as[l, j] * s_low
            total = s_low + d_low
            low_net = total - up
            terms = (net[j] - low_net, total, up, s_low)
            sums = terms if sums is None else tuple(a + b for a, b in zip(sums, terms))
            n_direct.append(s_low)
            n_diffuse.append(d_low)
            n_net.append(low_net)
        for f in range(4):
            acc[f, l] += sums[f]
        return tuple(n_direct), tuple(n_diffuse), tuple(n_net)

    lax.fori_loop(0, levels, downward, (direct0, diffuse0, net0), unroll=DOWN_UNROLL)

    @pl.when(chunk == pl.num_programs(0) - 1)
    def _():
        lit = register_order(lit_ref[...]).astype(jnp.float32)

        def body(l, c):
            heat_ref[l] = acc[0, l] * lit * (float(levels) / jnp.full((8, 128), mass_s[l]))
            return c

        lax.fori_loop(0, levels, body, 0, unroll=4)


def radiation(prognostic, daylit, cos_zenith, albedo, optics):
    fields, levels, cells_x, cells_y = prognostic.shape
    g_points = optics[1].shape[1]
    smem = pl.BlockSpec(memory_space=pltpu.SMEM)
    vec = pl.BlockSpec((8, 128), lambda c: (0, 0))
    field_specs = [
        pl.BlockSpec(
            (1, levels, cells_x, cells_y), lambda c, f=f: (f, 0, 0, 0), pipeline_mode=pl.Buffered(1)
        )
        for f in range(1, 4)
    ]
    kept = pltpu.VMEM((levels, G_CHUNK, 8, 128), jnp.float32)
    return pl.pallas_call(
        radiation_kernel,
        grid=(g_points // G_CHUNK,),
        in_specs=[smem] * 6 + [vec] * 3 + field_specs,
        out_specs=[
            pl.BlockSpec(memory_space=pl.ANY),
            pl.BlockSpec((levels, 8, 128), lambda c: (0, 0, 0)),
            pl.BlockSpec((4, levels, 8, 128), lambda c: (0, 0, 0, 0)),
        ],
        out_shape=[
            jax.ShapeDtypeStruct(prognostic.shape, jnp.float32),
            jax.ShapeDtypeStruct((levels, 8, 128), jnp.float32),
            jax.ShapeDtypeStruct((4, levels, 8, 128), jnp.float32),
        ],
        scratch_shapes=[pltpu.VMEM((3, levels, 8, 128), jnp.float32), kept, kept, kept, kept, kept],
        compiler_params=pltpu.CompilerParams(vmem_limit_bytes=SOLVE_VMEM),
        name="radiation",
    )(
        *optics,
        daylit.reshape(8, 128), cos_zenith.reshape(8, 128), albedo.reshape(8, 128),
        prognostic, prognostic, prognostic,
    )


def expand_kernel(lit_ref, heat_ref, acc_ref, out_ref):
    lit = register_order(lit_ref[...]).astype(jnp.float32)

    def body(l, c):
        for f in range(4):
            value = heat_ref[l] if f == 0 else acc_ref[f, l] * lit
            for xh in range(2):
                for yh in range(2):
                    out_ref[f, l, 8 * xh : 8 * xh + 8, 128 * yh : 128 * yh + 128] = spread_part(
                        value, xh, yh
                    )
        return c

    lax.fori_loop(0, heat_ref.shape[0], body, 0, unroll=2)


def expand(daylit, heat, fluxes, shape):
    fields, levels, cells_x, cells_y = shape
    block = EXPAND_BLOCK
    return pl.pallas_call(
        expand_kernel,
        grid=(levels // block,),
        in_specs=[
            pl.BlockSpec((8, 128), lambda i: (0, 0)),
            pl.BlockSpec((block, 8, 128), lambda i: (i, 0, 0)),
            pl.BlockSpec((4, block, 8, 128), lambda i: (0, i, 0, 0)),
        ],
        out_specs=pl.BlockSpec((fields, block, cells_x, cells_y), lambda i: (0, i, 0, 0)),
        out_shape=jax.ShapeDtypeStruct(shape, jnp.float32),
        compiler_params=pltpu.CompilerParams(vmem_limit_bytes=SMALL_VMEM),
        name="expand",
    )(daylit.reshape(8, 128), heat, fluxes)


def inverse(value):
    return pl.reciprocal(value, approx=False)


def wall_mask(shape):
    return (lax.broadcasted_iota(jnp.int32, shape, len(shape) - 1) > 0).astype(jnp.float32)


def upwind(low, high, face):
    return jnp.maximum(face, 0.0) * low + jnp.minimum(face, 0.0) * high


def across_y(value, face):
    flux = upwind(pltpu.roll(value, 1, 1), value, face)
    return pltpu.roll(flux, value.shape[1] - 1, 1) - flux


def edges_kernel(prog_ref, cour_ref, right_ref, left_ref, rows):
    fields, block, cells_x, cells_y = prog_ref.shape
    last = cells_x - 1
    picks = [(prog_ref, f, x) for x in (last, last - 1, 0, 1) for f in range(fields)]
    picks += [(cour_ref, 0, last), (cour_ref, 0, 1), (cour_ref, 0, 0), (cour_ref, 1, last), (cour_ref, 1, 0)]
    for l in range(block):
        for k, (ref, f, x) in enumerate(picks):
            rows[k, l : l + 1, :] = ref[f, l, x : x + 1, :]
    base = 4 * fields
    u_last, u_one, u_zero = rows[base], rows[base + 1], rows[base + 2]
    wall = wall_mask((block, cells_y))
    v_last, v_zero = rows[base + 3] * wall, rows[base + 4] * wall
    for f in range(fields):
        end, inner = rows[f], rows[fields + f]
        right_ref[f] = end
        right_ref[fields + f] = end + upwind(inner, end, u_last) - across_y(end, v_last)
        start, inner = rows[2 * fields + f], rows[3 * fields + f]
        left_ref[f] = start
        left_ref[fields + f] = start - upwind(start, inner, u_one) - across_y(start, v_zero)
    left_ref[2 * fields] = u_zero


def edges(prognostic, courant):
    fields, levels, cells_x, cells_y = prognostic.shape
    block = EDGE_BLOCK
    return pl.pallas_call(
        edges_kernel,
        grid=(levels // block,),
        in_specs=[
            pl.BlockSpec((fields, block, cells_x, cells_y), lambda i: (0, i, 0, 0)),
            pl.BlockSpec((2, block, cells_x, cells_y), lambda i: (0, i, 0, 0)),
        ],
        out_specs=[
            pl.BlockSpec((2 * fields, block, cells_y), lambda i: (0, i, 0)),
            pl.BlockSpec((2 * fields + 1, block, cells_y), lambda i: (0, i, 0)),
        ],
        out_shape=[
            jax.ShapeDtypeStruct((2 * fields, levels, cells_y), jnp.float32),
            jax.ShapeDtypeStruct((2 * fields + 1, levels, cells_y), jnp.float32),
        ],
        scratch_shapes=[pltpu.VMEM((4 * fields + 5, block, cells_y), jnp.float32)],
        compiler_params=pltpu.CompilerParams(vmem_limit_bytes=SMALL_VMEM),
        name="edges",
    )(prognostic, courant)


def no_edges(prognostic):
    fields, levels, _, cells_y = prognostic.shape
    return pl.pallas_call(
        lambda right_ref, left_ref: None,
        out_specs=[pl.BlockSpec(memory_space=pl.ANY)] * 2,
        out_shape=[
            jax.ShapeDtypeStruct((2 * fields, levels, cells_y), jnp.float32),
            jax.ShapeDtypeStruct((2 * fields + 1, levels, cells_y), jnp.float32),
        ],
        compiler_params=pltpu.CompilerParams(vmem_limit_bytes=SMALL_VMEM),
        name="no_edges",
    )()


def pass_one_kernel(prog_ref, cour_ref, first_ref, heat_ref, acc_ref):
    fields, block, cells_x, cells_y = prog_ref.shape
    shape = (cells_x, cells_y)
    wall = wall_mask(shape)
    inside = (lax.broadcasted_iota(jnp.int32, shape, 0) > 0).astype(jnp.float32)

    def body(l, c):
        u = cour_ref[0, l] * inside
        v = cour_ref[1, l] * wall
        up, um = jnp.maximum(u, 0.0), jnp.minimum(u, 0.0)
        vp, vm = jnp.maximum(v, 0.0), jnp.minimum(v, 0.0)
        for f in range(fields):
            p = prog_ref[f, l]
            flux = up * pltpu.roll(p, 1, 0) + um * p
            flux_y = vp * pltpu.roll(p, 1, 1) + vm * p
            first_ref[f, l] = (
                p
                - (pltpu.roll(flux, cells_x - 1, 0) - flux)
                - (pltpu.roll(flux_y, cells_y - 1, 1) - flux_y)
            )
        return c

    lax.fori_loop(0, block, body, 0, unroll=ONE_UNROLL)


def pass_one(prognostic, courant):
    fields, levels, cells_x, cells_y = prognostic.shape
    block = ONE_BLOCK
    plane = pl.BlockSpec((fields, block, cells_x, cells_y), lambda i: (0, i, 0, 0))
    return pl.pallas_call(
        pass_one_kernel,
        grid=(levels // block,),
        in_specs=[plane, pl.BlockSpec((2, block, cells_x, cells_y), lambda i: (0, i, 0, 0))],
        out_specs=[plane, pl.BlockSpec(memory_space=pl.ANY), pl.BlockSpec(memory_space=pl.ANY)],
        out_shape=[
            jax.ShapeDtypeStruct(prognostic.shape, jnp.float32),
            jax.ShapeDtypeStruct((levels, 8, 128), jnp.float32),
            jax.ShapeDtypeStruct((4, levels, 8, 128), jnp.float32),
        ],
        compiler_params=pltpu.CompilerParams(vmem_limit_bytes=SMALL_VMEM),
        name="pass_one",
    )(prognostic, courant)


def pass_two_kernel(
    first_ref, cour_ref, my_right, my_left, left_ref, right_ref,
    out_ref, row_m1, row_0, row_15, flux_16,
):
    fields, block, cells_x, cells_y = first_ref.shape
    shape = (cells_x, cells_y)
    last = cells_x - 1
    row = lax.broadcasted_iota(jnp.int32, shape, 0)
    wall = wall_mask(shape)
    is_first, is_last = row == 0, row == last

    u0, u16 = my_left[2 * fields], right_ref[2 * fields]
    gain = jnp.abs(u16) - u16 * u16
    for f in range(fields):
        begin = upwind(left_ref[f], my_left[f], u0)
        end = upwind(my_right[f], right_ref[f], u16)
        row_m1[f] = left_ref[fields + f] - begin
        row_0[f] = my_left[fields + f] + begin
        lo = my_right[fields + f] - end
        hi = right_ref[fields + f] + end
        row_15[f] = lo
        speed = gain * (hi - lo) * inverse(hi + lo)
        flux_16[f] = upwind(lo, hi, speed)

    def body(l, c):
        u = cour_ref[0, l]
        v = cour_ref[1, l] * wall
        gain_x = jnp.abs(u) - u * u
        gain_y = jnp.abs(v) - v * v
        one = pl.ds(l, 1)
        for f in range(fields):
            p = first_ref[f, l]
            p = jnp.where(is_first, row_0[f, one, :], jnp.where(is_last, row_15[f, one, :], p))
            lo = jnp.where(is_first, row_m1[f, one, :], pltpu.roll(p, 1, 0))
            flux = upwind(lo, p, gain_x * (p - lo) * inverse(p + lo))
            lo = pltpu.roll(p, 1, 1)
            flux_y = upwind(lo, p, gain_y * (p - lo) * inverse(p + lo))
            beyond = jnp.where(is_last, flux_16[f, one, :], pltpu.roll(flux, last, 0))
            out_ref[f, l] = p - (beyond - flux) - (pltpu.roll(flux_y, cells_y - 1, 1) - flux_y)
        return c

    lax.fori_loop(0, block, body, 0, unroll=TWO_UNROLL)


def pass_two(first, courant, my_right, my_left, left, right):
    fields, levels, cells_x, cells_y = first.shape
    block = TWO_BLOCK
    plane = pl.BlockSpec((fields, block, cells_x, cells_y), lambda i: (0, i, 0, 0))
    rows = pltpu.VMEM((fields, block, cells_y), jnp.float32)
    return pl.pallas_call(
        pass_two_kernel,
        grid=(levels // block,),
        in_specs=[
            plane,
            pl.BlockSpec((2, block, cells_x, cells_y), lambda i: (0, i, 0, 0)),
        ]
        + [
            pl.BlockSpec((edge.shape[0], block, cells_y), lambda i: (0, i, 0))
            for edge in (my_right, my_left, left, right)
        ],
        out_specs=plane,
        out_shape=jax.ShapeDtypeStruct(first.shape, jnp.float32),
        scratch_shapes=[rows, rows, rows, rows],
        compiler_params=pltpu.CompilerParams(vmem_limit_bytes=SMALL_VMEM),
        name="pass_two",
    )(first, courant, my_right, my_left, left, right)


def warm_kernel(field_ref, heat_ref, out_ref):
    block = field_ref.shape[1]
    start = pl.program_id(0) * block

    def body(l, c):
        packed = heat_ref[start + l] * STEP_LENGTH
        for xh in range(2):
            for yh in range(2):
                part = (0, l, slice(8 * xh, 8 * xh + 8), slice(128 * yh, 128 * yh + 128))
                out_ref[part] = field_ref[part] + spread_part(packed, xh, yh)
        return c

    lax.fori_loop(0, block, body, 0, unroll=4)


def warm(fields, heat):
    _, levels, cells_x, cells_y = fields.shape
    block = WARM_BLOCK
    spec = pl.BlockSpec((1, block, cells_x, cells_y), lambda i: (0, i, 0, 0))
    return pl.pallas_call(
        warm_kernel,
        grid=(levels // block,),
        in_specs=[spec, pl.BlockSpec(memory_space=pltpu.VMEM)],
        out_specs=spec,
        out_shape=jax.ShapeDtypeStruct(fields.shape, jnp.float32),
        input_output_aliases={0: 0},
        compiler_params=pltpu.CompilerParams(vmem_limit_bytes=SMALL_VMEM),
        name="warm",
    )(fields, heat)


def per_device(prognostic, courant, daylit, cos_zenith, albedo, *optics):
    dynamics = lax.axis_index("grp") == 0
    tiles = lax.axis_size("tile")
    to_right, to_left = lax.cond(
        dynamics, lambda: edges(prognostic, courant), lambda: no_edges(prognostic)
    )
    left = lax.ppermute(to_right, ("grp", "tile"), [(i, (i + 1) % tiles) for i in range(tiles)])
    right = lax.ppermute(to_left, ("grp", "tile"), [((i + 1) % tiles, i) for i in range(tiles)])
    first, heat, fluxes = lax.cond(
        dynamics,
        lambda: pass_one(prognostic, courant),
        lambda: radiation(prognostic, daylit, cos_zenith, albedo, optics),
    )
    heat_in = lax.ppermute(heat, "grp", [(1, 0)])
    fields = lax.cond(
        dynamics,
        lambda left, right: pass_two(first, courant, to_right, to_left, left, right),
        lambda left, right: expand(daylit, heat, fluxes, prognostic.shape),
        left, right,
    )
    return warm(fields, heat_in)[None]


def solution(mesh):
    column = P("tile")
    plane = P(None, None, "tile", None)
    return jax.shard_map(
        per_device,
        mesh=mesh,
        in_specs=(plane, plane, column, column, column) + (P(),) * 6,
        out_specs=P("grp", None, None, "tile", None),
        check_vma=False,
    )
```

```python
import functools

import jax
import jax.numpy as jnp
from jax import lax
from jax.experimental import pallas as pl
from jax.experimental.pallas import tpu as pltpu
from jax.sharding import PartitionSpec as P

COARSEN = 4
DIFFUSIVITY = 1.66
STEP_LENGTH = 1.0
LOG2E = 1.4426950408889634
G_CHUNK = 8
UP_UNROLL = 2
DOWN_UNROLL = 1
EDGE_BLOCK = 16
ONE_BLOCK = 16
ONE_UNROLL = 4
TWO_BLOCK = 16
TWO_UNROLL = 4
EXPAND_BLOCK = 16
WARM_BLOCK = 32
WARM_UNROLL = 8
COARSE_UNROLL = 8
COARSE_CHUNKS = 4
SOLVE_VMEM = 24 * 1024 * 1024
SMALL_VMEM = 16 * 1024 * 1024


def pack_means(tile):
    sub = lax.broadcasted_iota(jnp.int32, (8, 128), 0) % 4
    packed = None
    for xh in range(2):
        for yh in range(2):
            part = tile[8 * xh : 8 * xh + 8, 128 * yh : 128 * yh + 128]
            part = part + pltpu.roll(part, 7, 0)
            part = part + pltpu.roll(part, 6, 0)
            k = 2 * xh + yh
            if k:
                part = pltpu.roll(part, k, 0)
            packed = part if packed is None else jnp.where(sub == k, part, packed)
    return packed * (1.0 / COARSEN)


def spread_part(packed, xh, yh):
    k = 2 * xh + yh
    low = jnp.broadcast_to(packed[k : k + 1], (8, 128))
    high = jnp.broadcast_to(packed[4 + k : 5 + k], (8, 128))
    return jnp.where(lax.broadcasted_iota(jnp.int32, (8, 128), 0) < 4, low, high)


def spread_row(ref, l, xh, yh):
    k = 2 * xh + yh
    low = jnp.broadcast_to(ref[l, k : k + 1, :], (8, 128))
    high = jnp.broadcast_to(ref[l, 4 + k : 5 + k, :], (8, 128))
    return jnp.where(lax.broadcasted_iota(jnp.int32, (8, 128), 0) < 4, low, high)


def register_order(rows):
    return jnp.concatenate([rows[0:2], rows[4:6], rows[2:4], rows[6:8]], axis=0)


def radiation_kernel(
    mass_s, vap_s, oz_s, ext_s, alb_s, sol_s,
    lit_ref, cos_ref, ground_ref, prog_ref,
    unused_ref, heat_ref, acc,
    fine, sems, coarse, k_tdir, k_a, k_b, k_ad, k_as,
):
    chunk = pl.program_id(0)
    levels = acc.shape[1]

    @pl.when(chunk == 0)
    def _():
        part = levels // COARSE_CHUNKS
        copies = []
        for c in range(COARSE_CHUNKS):
            here = pl.ds(c * part, part)
            copies.append(
                pltpu.make_async_copy(prog_ref.at[pl.ds(1, 3), here], fine.at[:, here], sems.at[c])
            )
            copies[-1].start()

        def body(l, c):
            scale = mass_s[l]
            for f in range(3):
                coarse[f, l] = pack_means(fine[f, l]) * scale
            for f in range(4):
                acc[f, l] = jnp.zeros((8, 128), jnp.float32)
            return c

        for c in range(COARSE_CHUNKS):
            copies[c].wait()
            lax.fori_loop(c * part, (c + 1) * part, body, 0, unroll=COARSE_UNROLL)

    cosine = register_order(cos_ref[...])
    ground = register_order(ground_ref[...])
    dir_rate = -LOG2E / cosine
    dif_rate = -LOG2E * DIFFUSIVITY
    g0 = chunk * G_CHUNK
    oz = [oz_s[g0 + j] for j in range(G_CHUNK)]
    ext = [ext_s[g0 + j] for j in range(G_CHUNK)]
    half_alb = [0.5 * alb_s[g0 + j] for j in range(G_CHUNK)]

    def upward(i, carry):
        l = levels - 1 - i
        alb_dif, alb_dir = carry
        vapour, cloud, ozone = coarse[0, l], coarse[1, l], coarse[2, l]
        new_dif, new_dir = [], []
        for j in range(G_CHUNK):
            cloud_depth = cloud * ext[j]
            depth = (vapour * vap_s[l, g0 + j] + ozone * oz[j]) + cloud_depth
            half_w = (cloud_depth * half_alb[j]) * inverse(depth)
            t_dir = jnp.exp2(depth * dir_rate)
            t_dif = jnp.exp2(depth * dif_rate)
            t_sq = t_dif * t_dif
            r_dif = half_w * (1.0 - t_sq)
            s_dir = half_w * (1.0 - t_dir)
            den = inverse(1.0 - r_dif * alb_dif[j])
            through = alb_dir[j] * t_dir
            down = (s_dir + r_dif * through) * den
            k_tdir[l, j] = t_dir
            k_a[l, j] = t_dif * den
            k_b[l, j] = down
            k_ad[l, j] = alb_dif[j]
            k_as[l, j] = alb_dir[j]
            new_dir.append(s_dir + t_dif * (alb_dif[j] * down + through))
            new_dif.append(r_dif + t_sq * alb_dif[j] * den)
        return tuple(new_dif), tuple(new_dir)

    start = (ground,) * G_CHUNK
    _, top_dir = lax.fori_loop(0, levels, upward, (start, start), unroll=UP_UNROLL)

    direct0 = tuple(cosine * sol_s[g0 + j] for j in range(G_CHUNK))
    net0 = tuple(d - t * d for d, t in zip(direct0, top_dir))
    diffuse0 = tuple(jnp.zeros((8, 128), jnp.float32) for _ in range(G_CHUNK))

    def downward(l, carry):
        direct, diffuse, net = carry
        n_direct, n_diffuse, n_net = [], [], []
        sums = None
        for j in range(G_CHUNK):
            s_low = direct[j] * k_tdir[l, j]
            d_low = diffuse[j] * k_a[l, j] + direct[j] * k_b[l, j]
            up = k_ad[l, j] * d_low + k_as[l, j] * s_low
            total = s_low + d_low
            low_net = total - up
            terms = (net[j] - low_net, total, up, s_low)
            sums = terms if sums is None else tuple(a + b for a, b in zip(sums, terms))
            n_direct.append(s_low)
            n_diffuse.append(d_low)
            n_net.append(low_net)
        for f in range(4):
            acc[f, l] += sums[f]
        return tuple(n_direct), tuple(n_diffuse), tuple(n_net)

    lax.fori_loop(0, levels, downward, (direct0, diffuse0, net0), unroll=DOWN_UNROLL)

    @pl.when(chunk == pl.num_programs(0) - 1)
    def _():
        lit = register_order(lit_ref[...]).astype(jnp.float32)

        def body(l, c):
            heat_ref[l] = acc[0, l] * lit * (float(levels) / jnp.full((8, 128), mass_s[l]))
            return c

        lax.fori_loop(0, levels, body, 0, unroll=4)


def radiation(prognostic, daylit, cos_zenith, albedo, optics):
    fields, levels, cells_x, cells_y = prognostic.shape
    g_points = optics[1].shape[1]
    smem = pl.BlockSpec(memory_space=pltpu.SMEM)
    vec = pl.BlockSpec((8, 128), lambda c: (0, 0))
    kept = pltpu.VMEM((levels, G_CHUNK, 8, 128), jnp.float32)
    return pl.pallas_call(
        radiation_kernel,
        grid=(g_points // G_CHUNK,),
        in_specs=[smem] * 6 + [vec] * 3 + [pl.BlockSpec(memory_space=pl.ANY)],
        out_specs=[
            pl.BlockSpec(memory_space=pl.ANY),
            pl.BlockSpec((levels, 8, 128), lambda c: (0, 0, 0)),
            pl.BlockSpec((4, levels, 8, 128), lambda c: (0, 0, 0, 0)),
        ],
        out_shape=[
            jax.ShapeDtypeStruct(prognostic.shape, jnp.float32),
            jax.ShapeDtypeStruct((levels, 8, 128), jnp.float32),
            jax.ShapeDtypeStruct((4, levels, 8, 128), jnp.float32),
        ],
        scratch_shapes=[
            pltpu.VMEM((3, levels, cells_x, cells_y), jnp.float32),
            pltpu.SemaphoreType.DMA((COARSE_CHUNKS,)),
            pltpu.VMEM((3, levels, 8, 128), jnp.float32),
            kept, kept, kept, kept, kept,
        ],
        compiler_params=pltpu.CompilerParams(vmem_limit_bytes=SOLVE_VMEM),
        name="radiation",
    )(
        *optics,
        daylit.reshape(8, 128), cos_zenith.reshape(8, 128), albedo.reshape(8, 128),
        prognostic,
    )


def expand_kernel(lit_ref, heat_ref, acc_ref, out_ref):
    lit = register_order(lit_ref[...]).astype(jnp.float32)

    def body(l, c):
        for f in range(4):
            value = heat_ref[l] if f == 0 else acc_ref[f, l] * lit
            for xh in range(2):
                for yh in range(2):
                    out_ref[f, l, 8 * xh : 8 * xh + 8, 128 * yh : 128 * yh + 128] = spread_part(
                        value, xh, yh
                    )
        return c

    lax.fori_loop(0, heat_ref.shape[0], body, 0, unroll=2)


def expand(daylit, heat, fluxes, shape):
    fields, levels, cells_x, cells_y = shape
    block = EXPAND_BLOCK
    return pl.pallas_call(
        expand_kernel,
        grid=(levels // block,),
        in_specs=[
            pl.BlockSpec((8, 128), lambda i: (0, 0)),
            pl.BlockSpec((block, 8, 128), lambda i: (i, 0, 0)),
            pl.BlockSpec((4, block, 8, 128), lambda i: (0, i, 0, 0)),
        ],
        out_specs=pl.BlockSpec((fields, block, cells_x, cells_y), lambda i: (0, i, 0, 0)),
        out_shape=jax.ShapeDtypeStruct(shape, jnp.float32),
        compiler_params=pltpu.CompilerParams(vmem_limit_bytes=SMALL_VMEM),
        name="expand",
    )(daylit.reshape(8, 128), heat, fluxes)


def inverse(value):
    return pl.reciprocal(value, approx=False)


def wall_mask(shape):
    return (lax.broadcasted_iota(jnp.int32, shape, len(shape) - 1) > 0).astype(jnp.float32)


def upwind(low, high, face):
    return jnp.maximum(face, 0.0) * low + jnp.minimum(face, 0.0) * high


def across_y(value, face):
    flux = upwind(pltpu.roll(value, 1, 1), value, face)
    return pltpu.roll(flux, value.shape[1] - 1, 1) - flux


def edges_kernel(prog_ref, cour_ref, right_ref, left_ref, rows):
    fields, block, cells_x, cells_y = prog_ref.shape
    last = cells_x - 1
    picks = [(prog_ref, f, x) for x in (last, last - 1, 0, 1) for f in range(fields)]
    picks += [(cour_ref, 0, last), (cour_ref, 0, 1), (cour_ref, 0, 0), (cour_ref, 1, last), (cour_ref, 1, 0)]
    for l in range(block):
        for k, (ref, f, x) in enumerate(picks):
            rows[k, l : l + 1, :] = ref[f, l, x : x + 1, :]
    base = 4 * fields
    u_last, u_one, u_zero = rows[base], rows[base + 1], rows[base + 2]
    wall = wall_mask((block, cells_y))
    v_last, v_zero = rows[base + 3] * wall, rows[base + 4] * wall
    for f in range(fields):
        end, inner = rows[f], rows[fields + f]
        right_ref[f] = end
        right_ref[fields + f] = end + upwind(inner, end, u_last) - across_y(end, v_last)
        start, inner = rows[2 * fields + f], rows[3 * fields + f]
        left_ref[f] = start
        left_ref[fields + f] = start - upwind(start, inner, u_one) - across_y(start, v_zero)
    left_ref[2 * fields] = u_zero


def edges(prognostic, courant):
    fields, levels, cells_x, cells_y = prognostic.shape
    block = EDGE_BLOCK
    return pl.pallas_call(
        edges_kernel,
        grid=(levels // block,),
        in_specs=[
            pl.BlockSpec((fields, block, cells_x, cells_y), lambda i: (0, i, 0, 0)),
            pl.BlockSpec((2, block, cells_x, cells_y), lambda i: (0, i, 0, 0)),
        ],
        out_specs=[
            pl.BlockSpec((2 * fields, block, cells_y), lambda i: (0, i, 0)),
            pl.BlockSpec((2 * fields + 1, block, cells_y), lambda i: (0, i, 0)),
        ],
        out_shape=[
            jax.ShapeDtypeStruct((2 * fields, levels, cells_y), jnp.float32),
            jax.ShapeDtypeStruct((2 * fields + 1, levels, cells_y), jnp.float32),
        ],
        scratch_shapes=[pltpu.VMEM((4 * fields + 5, block, cells_y), jnp.float32)],
        compiler_params=pltpu.CompilerParams(vmem_limit_bytes=SMALL_VMEM),
        name="edges",
    )(prognostic, courant)


def no_edges(prognostic):
    fields, levels, _, cells_y = prognostic.shape
    return pl.pallas_call(
        lambda right_ref, left_ref: None,
        out_specs=[pl.BlockSpec(memory_space=pl.ANY)] * 2,
        out_shape=[
            jax.ShapeDtypeStruct((2 * fields, levels, cells_y), jnp.float32),
            jax.ShapeDtypeStruct((2 * fields + 1, levels, cells_y), jnp.float32),
        ],
        compiler_params=pltpu.CompilerParams(vmem_limit_bytes=SMALL_VMEM),
        name="no_edges",
    )()


def pass_one_kernel(prog_ref, cour_ref, first_ref, heat_ref, acc_ref):
    fields, block, cells_x, cells_y = prog_ref.shape
    shape = (cells_x, cells_y)
    wall = wall_mask(shape)
    inside = (lax.broadcasted_iota(jnp.int32, shape, 0) > 0).astype(jnp.float32)

    def body(l, c):
        u = cour_ref[0, l] * inside
        v = cour_ref[1, l] * wall
        up, um = jnp.maximum(u, 0.0), jnp.minimum(u, 0.0)
        vp, vm = jnp.maximum(v, 0.0), jnp.minimum(v, 0.0)
        for f in range(fields):
            p = prog_ref[f, l]
            flux = up * pltpu.roll(p, 1, 0) + um * p
            flux_y = vp * pltpu.roll(p, 1, 1) + vm * p
            first_ref[f, l] = (
                p
                - (pltpu.roll(flux, cells_x - 1, 0) - flux)
                - (pltpu.roll(flux_y, cells_y - 1, 1) - flux_y)
            )
        return c

    lax.fori_loop(0, block, body, 0, unroll=ONE_UNROLL)


def pass_one(prognostic, courant):
    fields, levels, cells_x, cells_y = prognostic.shape
    block = ONE_BLOCK
    plane = pl.BlockSpec((fields, block, cells_x, cells_y), lambda i: (0, i, 0, 0))
    return pl.pallas_call(
        pass_one_kernel,
        grid=(levels // block,),
        in_specs=[plane, pl.BlockSpec((2, block, cells_x, cells_y), lambda i: (0, i, 0, 0))],
        out_specs=[plane, pl.BlockSpec(memory_space=pl.ANY), pl.BlockSpec(memory_space=pl.ANY)],
        out_shape=[
            jax.ShapeDtypeStruct(prognostic.shape, jnp.float32),
            jax.ShapeDtypeStruct((levels, 8, 128), jnp.float32),
            jax.ShapeDtypeStruct((4, levels, 8, 128), jnp.float32),
        ],
        compiler_params=pltpu.CompilerParams(vmem_limit_bytes=SMALL_VMEM),
        name="pass_one",
    )(prognostic, courant)


def pass_two_kernel(
    first_ref, cour_ref, my_right, my_left, left_ref, right_ref,
    out_ref, row_m1, row_0, row_15, flux_16,
):
    fields, block, cells_x, cells_y = first_ref.shape
    shape = (cells_x, cells_y)
    last = cells_x - 1
    row = lax.broadcasted_iota(jnp.int32, shape, 0)
    wall = wall_mask(shape)
    is_first, is_last = row == 0, row == last

    u0, u16 = my_left[2 * fields], right_ref[2 * fields]
    gain = jnp.abs(u16) - u16 * u16
    for f in range(fields):
        begin = upwind(left_ref[f], my_left[f], u0)
        end = upwind(my_right[f], right_ref[f], u16)
        row_m1[f] = left_ref[fields + f] - begin
        row_0[f] = my_left[fields + f] + begin
        lo = my_right[fields + f] - end
        hi = right_ref[fields + f] + end
        row_15[f] = lo
        speed = gain * (hi - lo) * inverse(hi + lo)
        flux_16[f] = upwind(lo, hi, speed)

    def body(l, c):
        u = cour_ref[0, l]
        v = cour_ref[1, l] * wall
        gain_x = jnp.abs(u) - u * u
        gain_y = jnp.abs(v) - v * v
        one = pl.ds(l, 1)
        for f in range(fields):
            p = first_ref[f, l]
            p = jnp.where(is_first, row_0[f, one, :], jnp.where(is_last, row_15[f, one, :], p))
            lo = jnp.where(is_first, row_m1[f, one, :], pltpu.roll(p, 1, 0))
            flux = upwind(lo, p, gain_x * (p - lo) * inverse(p + lo))
            lo = pltpu.roll(p, 1, 1)
            flux_y = upwind(lo, p, gain_y * (p - lo) * inverse(p + lo))
            beyond = jnp.where(is_last, flux_16[f, one, :], pltpu.roll(flux, last, 0))
            out_ref[f, l] = p - (beyond - flux) - (pltpu.roll(flux_y, cells_y - 1, 1) - flux_y)
        return c

    lax.fori_loop(0, block, body, 0, unroll=TWO_UNROLL)


def pass_two(first, courant, my_right, my_left, left, right):
    fields, levels, cells_x, cells_y = first.shape
    block = TWO_BLOCK
    plane = pl.BlockSpec((fields, block, cells_x, cells_y), lambda i: (0, i, 0, 0))
    rows = pltpu.VMEM((fields, block, cells_y), jnp.float32)
    return pl.pallas_call(
        pass_two_kernel,
        grid=(levels // block,),
        in_specs=[
            plane,
            pl.BlockSpec((2, block, cells_x, cells_y), lambda i: (0, i, 0, 0)),
        ]
        + [
            pl.BlockSpec((edge.shape[0], block, cells_y), lambda i: (0, i, 0))
            for edge in (my_right, my_left, left, right)
        ],
        out_specs=plane,
        out_shape=jax.ShapeDtypeStruct(first.shape, jnp.float32),
        scratch_shapes=[rows, rows, rows, rows],
        compiler_params=pltpu.CompilerParams(vmem_limit_bytes=SMALL_VMEM),
        name="pass_two",
    )(first, courant, my_right, my_left, left, right)


def warm_kernel(field_ref, heat_ref, out_ref):
    block = field_ref.shape[1]
    start = pl.program_id(0) * block

    def body(l, c):
        for xh in range(2):
            for yh in range(2):
                part = (0, l, slice(8 * xh, 8 * xh + 8), slice(128 * yh, 128 * yh + 128))
                heating = spread_row(heat_ref, start + l, xh, yh)
                out_ref[part] = field_ref[part] + STEP_LENGTH * heating
        return c

    lax.fori_loop(0, block, body, 0, unroll=WARM_UNROLL)


def warm(fields, heat):
    _, levels, cells_x, cells_y = fields.shape
    block = WARM_BLOCK
    spec = pl.BlockSpec((1, block, cells_x, cells_y), lambda i: (0, i, 0, 0))
    return pl.pallas_call(
        warm_kernel,
        grid=(levels // block,),
        in_specs=[spec, pl.BlockSpec(memory_space=pltpu.VMEM)],
        out_specs=spec,
        out_shape=jax.ShapeDtypeStruct(fields.shape, jnp.float32),
        input_output_aliases={0: 0},
        compiler_params=pltpu.CompilerParams(vmem_limit_bytes=SMALL_VMEM),
        name="warm",
    )(fields, heat)


def per_device(prognostic, courant, daylit, cos_zenith, albedo, *optics):
    dynamics = lax.axis_index("grp") == 0
    tiles = lax.axis_size("tile")
    to_right, to_left = lax.cond(
        dynamics, lambda: edges(prognostic, courant), lambda: no_edges(prognostic)
    )
    left = lax.ppermute(to_right, ("grp", "tile"), [(i, (i + 1) % tiles) for i in range(tiles)])
    right = lax.ppermute(to_left, ("grp", "tile"), [((i + 1) % tiles, i) for i in range(tiles)])
    first, heat, fluxes = lax.cond(
        dynamics,
        lambda: pass_one(prognostic, courant),
        lambda: radiation(prognostic, daylit, cos_zenith, albedo, optics),
    )
    heat_in = lax.ppermute(heat, "grp", [(1, 0)])
    fields = lax.cond(
        dynamics,
        lambda left, right: pass_two(first, courant, to_right, to_left, left, right),
        lambda left, right: expand(daylit, heat, fluxes, prognostic.shape),
        left, right,
    )
    return warm(fields, heat_in)[None]


def solution(mesh):
    column = P("tile")
    plane = P(None, None, "tile", None)
    return jax.shard_map(
        per_device,
        mesh=mesh,
        in_specs=(plane, plane, column, column, column) + (P(),) * 6,
        out_specs=P("grp", None, None, "tile", None),
        check_vma=False,
    )
```

```python
import functools

import jax
import jax.numpy as jnp
from jax import lax
from jax.experimental import pallas as pl
from jax.experimental.pallas import tpu as pltpu
from jax.sharding import PartitionSpec as P

COARSEN = 4
DIFFUSIVITY = 1.66
STEP_LENGTH = 1.0
LOG2E = 1.4426950408889634
G_CHUNK = 8
UP_UNROLL = 4
DOWN_UNROLL = 4
EDGE_BLOCK = 32
ONE_BLOCK = 16
ONE_UNROLL = 4
TWO_BLOCK = 16
TWO_UNROLL = 4
EXPAND_BLOCK = 16
WARM_BLOCK = 32
WARM_UNROLL = 8
COARSE_UNROLL = 8
COARSE_CHUNKS = 4
SOLVE_VMEM = 24 * 1024 * 1024
SMALL_VMEM = 16 * 1024 * 1024


def pack_means(tile):
    sub = lax.broadcasted_iota(jnp.int32, (8, 128), 0) % 4
    packed = None
    for xh in range(2):
        for yh in range(2):
            part = tile[8 * xh : 8 * xh + 8, 128 * yh : 128 * yh + 128]
            part = part + pltpu.roll(part, 7, 0)
            part = part + pltpu.roll(part, 6, 0)
            k = 2 * xh + yh
            if k:
                part = pltpu.roll(part, k, 0)
            packed = part if packed is None else jnp.where(sub == k, part, packed)
    return packed * (1.0 / COARSEN)


def spread_part(packed, xh, yh):
    k = 2 * xh + yh
    low = jnp.broadcast_to(packed[k : k + 1], (8, 128))
    high = jnp.broadcast_to(packed[4 + k : 5 + k], (8, 128))
    return jnp.where(lax.broadcasted_iota(jnp.int32, (8, 128), 0) < 4, low, high)


def spread_row(ref, l, xh, yh):
    k = 2 * xh + yh
    low = jnp.broadcast_to(ref[l, k : k + 1, :], (8, 128))
    high = jnp.broadcast_to(ref[l, 4 + k : 5 + k, :], (8, 128))
    return jnp.where(lax.broadcasted_iota(jnp.int32, (8, 128), 0) < 4, low, high)


def register_order(rows):
    return jnp.concatenate([rows[0:2], rows[4:6], rows[2:4], rows[6:8]], axis=0)


def radiation_kernel(
    mass_s, vap_s, oz_s, ext_s, alb_s, sol_s,
    lit_ref, cos_ref, ground_ref, prog_ref,
    unused_ref, heat_ref, acc,
    fine, sems, coarse, k_tdir, k_a, k_b, k_ad, k_as,
):
    chunk = pl.program_id(0)
    levels = acc.shape[1]

    @pl.when(chunk == 0)
    def _():
        part = levels // COARSE_CHUNKS
        copies = []
        for c in range(COARSE_CHUNKS):
            here = pl.ds(c * part, part)
            copies.append(
                pltpu.make_async_copy(prog_ref.at[pl.ds(1, 3), here], fine.at[:, here], sems.at[c])
            )
            copies[-1].start()

        def body(l, c):
            scale = mass_s[l]
            for f in range(3):
                coarse[f, l] = pack_means(fine[f, l]) * scale
            for f in range(4):
                acc[f, l] = jnp.zeros((8, 128), jnp.float32)
            return c

        for c in range(COARSE_CHUNKS):
            copies[c].wait()
            lax.fori_loop(c * part, (c + 1) * part, body, 0, unroll=COARSE_UNROLL)

    cosine = register_order(cos_ref[...])
    ground = register_order(ground_ref[...])
    dir_rate = -LOG2E / cosine
    dif_rate = -LOG2E * DIFFUSIVITY
    g0 = chunk * G_CHUNK
    oz = [oz_s[g0 + j] for j in range(G_CHUNK)]
    ext = [ext_s[g0 + j] for j in range(G_CHUNK)]
    half_alb = [0.5 * alb_s[g0 + j] for j in range(G_CHUNK)]

    def upward(i, carry):
        l = levels - 1 - i
        alb_dif, alb_dir = carry
        vapour, cloud, ozone = coarse[0, l], coarse[1, l], coarse[2, l]
        new_dif, new_dir = [], []
        for j in range(G_CHUNK):
            cloud_depth = cloud * ext[j]
            depth = (vapour * vap_s[l, g0 + j] + ozone * oz[j]) + cloud_depth
            half_w = (cloud_depth * half_alb[j]) * inverse(depth)
            t_dir = jnp.exp2(depth * dir_rate)
            t_dif = jnp.exp2(depth * dif_rate)
            t_sq = t_dif * t_dif
            r_dif = half_w * (1.0 - t_sq)
            s_dir = half_w * (1.0 - t_dir)
            den = inverse(1.0 - r_dif * alb_dif[j])
            through = alb_dir[j] * t_dir
            down = (s_dir + r_dif * through) * den
            k_tdir[l, j] = t_dir
            k_a[l, j] = t_dif * den
            k_b[l, j] = down
            k_ad[l, j] = alb_dif[j]
            k_as[l, j] = alb_dir[j]
            new_dir.append(s_dir + t_dif * (alb_dif[j] * down + through))
            new_dif.append(r_dif + t_sq * alb_dif[j] * den)
        return tuple(new_dif), tuple(new_dir)

    start = (ground,) * G_CHUNK
    _, top_dir = lax.fori_loop(0, levels, upward, (start, start), unroll=UP_UNROLL)

    direct0 = tuple(cosine * sol_s[g0 + j] for j in range(G_CHUNK))
    net0 = tuple(d - t * d for d, t in zip(direct0, top_dir))
    diffuse0 = tuple(jnp.zeros((8, 128), jnp.float32) for _ in range(G_CHUNK))

    def downward(l, carry):
        direct, diffuse, net = carry
        n_direct, n_diffuse, n_net = [], [], []
        sums = None
        for j in range(G_CHUNK):
            s_low = direct[j] * k_tdir[l, j]
            d_low = diffuse[j] * k_a[l, j] + direct[j] * k_b[l, j]
            up = k_ad[l, j] * d_low + k_as[l, j] * s_low
            total = s_low + d_low
            low_net = total - up
            terms = (net[j] - low_net, total, up, s_low)
            sums = terms if sums is None else tuple(a + b for a, b in zip(sums, terms))
            n_direct.append(s_low)
            n_diffuse.append(d_low)
            n_net.append(low_net)
        for f in range(4):
            acc[f, l] += sums[f]
        return tuple(n_direct), tuple(n_diffuse), tuple(n_net)

    lax.fori_loop(0, levels, downward, (direct0, diffuse0, net0), unroll=DOWN_UNROLL)

    @pl.when(chunk == pl.num_programs(0) - 1)
    def _():
        lit = register_order(lit_ref[...]).astype(jnp.float32)

        def body(l, c):
            heat_ref[l] = acc[0, l] * lit * (float(levels) / jnp.full((8, 128), mass_s[l]))
            return c

        lax.fori_loop(0, levels, body, 0, unroll=4)


def radiation(prognostic, daylit, cos_zenith, albedo, optics):
    fields, levels, cells_x, cells_y = prognostic.shape
    g_points = optics[1].shape[1]
    smem = pl.BlockSpec(memory_space=pltpu.SMEM)
    vec = pl.BlockSpec((8, 128), lambda c: (0, 0))
    kept = pltpu.VMEM((levels, G_CHUNK, 8, 128), jnp.float32)
    return pl.pallas_call(
        radiation_kernel,
        grid=(g_points // G_CHUNK,),
        in_specs=[smem] * 6 + [vec] * 3 + [pl.BlockSpec(memory_space=pl.ANY)],
        out_specs=[
            pl.BlockSpec(memory_space=pl.ANY),
            pl.BlockSpec((levels, 8, 128), lambda c: (0, 0, 0)),
            pl.BlockSpec((4, levels, 8, 128), lambda c: (0, 0, 0, 0)),
        ],
        out_shape=[
            jax.ShapeDtypeStruct(prognostic.shape, jnp.float32),
            jax.ShapeDtypeStruct((levels, 8, 128), jnp.float32),
            jax.ShapeDtypeStruct((4, levels, 8, 128), jnp.float32),
        ],
        scratch_shapes=[
            pltpu.VMEM((3, levels, cells_x, cells_y), jnp.float32),
            pltpu.SemaphoreType.DMA((COARSE_CHUNKS,)),
            pltpu.VMEM((3, levels, 8, 128), jnp.float32),
            kept, kept, kept, kept, kept,
        ],
        compiler_params=pltpu.CompilerParams(vmem_limit_bytes=SOLVE_VMEM),
        name="radiation",
    )(
        *optics,
        daylit.reshape(8, 128), cos_zenith.reshape(8, 128), albedo.reshape(8, 128),
        prognostic,
    )


def expand_kernel(lit_ref, heat_ref, acc_ref, out_ref):
    lit = register_order(lit_ref[...]).astype(jnp.float32)

    def body(l, c):
        for f in range(4):
            value = heat_ref[l] if f == 0 else acc_ref[f, l] * lit
            for xh in range(2):
                for yh in range(2):
                    out_ref[f, l, 8 * xh : 8 * xh + 8, 128 * yh : 128 * yh + 128] = spread_part(
                        value, xh, yh
                    )
        return c

    lax.fori_loop(0, heat_ref.shape[0], body, 0, unroll=2)


def expand(daylit, heat, fluxes, shape):
    fields, levels, cells_x, cells_y = shape
    block = EXPAND_BLOCK
    return pl.pallas_call(
        expand_kernel,
        grid=(levels // block,),
        in_specs=[
            pl.BlockSpec((8, 128), lambda i: (0, 0)),
            pl.BlockSpec((block, 8, 128), lambda i: (i, 0, 0)),
            pl.BlockSpec((4, block, 8, 128), lambda i: (0, i, 0, 0)),
        ],
        out_specs=pl.BlockSpec((fields, block, cells_x, cells_y), lambda i: (0, i, 0, 0)),
        out_shape=jax.ShapeDtypeStruct(shape, jnp.float32),
        compiler_params=pltpu.CompilerParams(vmem_limit_bytes=SMALL_VMEM),
        name="expand",
    )(daylit.reshape(8, 128), heat, fluxes)


def inverse(value):
    return pl.reciprocal(value, approx=False)


def wall_mask(shape):
    return (lax.broadcasted_iota(jnp.int32, shape, len(shape) - 1) > 0).astype(jnp.float32)


def upwind(low, high, face):
    return jnp.maximum(face, 0.0) * low + jnp.minimum(face, 0.0) * high


def across_y(value, face):
    flux = upwind(pltpu.roll(value, 1, 1), value, face)
    return pltpu.roll(flux, value.shape[1] - 1, 1) - flux


def edges_kernel(prog_ref, cour_ref, right_ref, left_ref, rows):
    fields, block, cells_x, cells_y = prog_ref.shape
    last = cells_x - 1
    picks = [(prog_ref, f, x) for x in (last, last - 1, 0, 1) for f in range(fields)]
    picks += [(cour_ref, 0, last), (cour_ref, 0, 1), (cour_ref, 0, 0), (cour_ref, 1, last), (cour_ref, 1, 0)]
    for l in range(block):
        for k, (ref, f, x) in enumerate(picks):
            rows[k, l : l + 1, :] = ref[f, l, x : x + 1, :]
    base = 4 * fields
    u_last, u_one, u_zero = rows[base], rows[base + 1], rows[base + 2]
    wall = wall_mask((block, cells_y))
    v_last, v_zero = rows[base + 3] * wall, rows[base + 4] * wall
    for f in range(fields):
        end, inner = rows[f], rows[fields + f]
        right_ref[f] = end
        right_ref[fields + f] = end + upwind(inner, end, u_last) - across_y(end, v_last)
        start, inner = rows[2 * fields + f], rows[3 * fields + f]
        left_ref[f] = start
        left_ref[fields + f] = start - upwind(start, inner, u_one) - across_y(start, v_zero)
    left_ref[2 * fields] = u_zero


def edges(prognostic, courant):
    fields, levels, cells_x, cells_y = prognostic.shape
    block = EDGE_BLOCK
    return pl.pallas_call(
        edges_kernel,
        grid=(levels // block,),
        in_specs=[
            pl.BlockSpec((fields, block, cells_x, cells_y), lambda i: (0, i, 0, 0)),
            pl.BlockSpec((2, block, cells_x, cells_y), lambda i: (0, i, 0, 0)),
        ],
        out_specs=[
            pl.BlockSpec((2 * fields, block, cells_y), lambda i: (0, i, 0)),
            pl.BlockSpec((2 * fields + 1, block, cells_y), lambda i: (0, i, 0)),
        ],
        out_shape=[
            jax.ShapeDtypeStruct((2 * fields, levels, cells_y), jnp.float32),
            jax.ShapeDtypeStruct((2 * fields + 1, levels, cells_y), jnp.float32),
        ],
        scratch_shapes=[pltpu.VMEM((4 * fields + 5, block, cells_y), jnp.float32)],
        compiler_params=pltpu.CompilerParams(vmem_limit_bytes=SMALL_VMEM),
        name="edges",
    )(prognostic, courant)


def no_edges(prognostic):
    fields, levels, _, cells_y = prognostic.shape
    return pl.pallas_call(
        lambda right_ref, left_ref: None,
        out_specs=[pl.BlockSpec(memory_space=pl.ANY)] * 2,
        out_shape=[
            jax.ShapeDtypeStruct((2 * fields, levels, cells_y), jnp.float32),
            jax.ShapeDtypeStruct((2 * fields + 1, levels, cells_y), jnp.float32),
        ],
        compiler_params=pltpu.CompilerParams(vmem_limit_bytes=SMALL_VMEM),
        name="no_edges",
    )()


def pass_one_kernel(prog_ref, cour_ref, first_ref, heat_ref, acc_ref):
    fields, block, cells_x, cells_y = prog_ref.shape
    shape = (cells_x, cells_y)
    wall = wall_mask(shape)
    inside = (lax.broadcasted_iota(jnp.int32, shape, 0) > 0).astype(jnp.float32)

    def body(l, c):
        u = cour_ref[0, l] * inside
        v = cour_ref[1, l] * wall
        up, um = jnp.maximum(u, 0.0), jnp.minimum(u, 0.0)
        vp, vm = jnp.maximum(v, 0.0), jnp.minimum(v, 0.0)
        for f in range(fields):
            p = prog_ref[f, l]
            flux = up * pltpu.roll(p, 1, 0) + um * p
            flux_y = vp * pltpu.roll(p, 1, 1) + vm * p
            first_ref[f, l] = (
                p
                - (pltpu.roll(flux, cells_x - 1, 0) - flux)
                - (pltpu.roll(flux_y, cells_y - 1, 1) - flux_y)
            )
        return c

    lax.fori_loop(0, block, body, 0, unroll=ONE_UNROLL)


def pass_one(prognostic, courant):
    fields, levels, cells_x, cells_y = prognostic.shape
    block = ONE_BLOCK
    plane = pl.BlockSpec((fields, block, cells_x, cells_y), lambda i: (0, i, 0, 0))
    return pl.pallas_call(
        pass_one_kernel,
        grid=(levels // block,),
        in_specs=[plane, pl.BlockSpec((2, block, cells_x, cells_y), lambda i: (0, i, 0, 0))],
        out_specs=[plane, pl.BlockSpec(memory_space=pl.ANY), pl.BlockSpec(memory_space=pl.ANY)],
        out_shape=[
            jax.ShapeDtypeStruct(prognostic.shape, jnp.float32),
            jax.ShapeDtypeStruct((levels, 8, 128), jnp.float32),
            jax.ShapeDtypeStruct((4, levels, 8, 128), jnp.float32),
        ],
        compiler_params=pltpu.CompilerParams(vmem_limit_bytes=SMALL_VMEM),
        name="pass_one",
    )(prognostic, courant)


def pass_two_kernel(
    first_ref, cour_ref, my_right, my_left, left_ref, right_ref,
    out_ref, row_m1, row_0, row_15, flux_16,
):
    fields, block, cells_x, cells_y = first_ref.shape
    shape = (cells_x, cells_y)
    last = cells_x - 1
    row = lax.broadcasted_iota(jnp.int32, shape, 0)
    wall = wall_mask(shape)
    is_first, is_last = row == 0, row == last

    u0, u16 = my_left[2 * fields], right_ref[2 * fields]
    gain = jnp.abs(u16) - u16 * u16
    for f in range(fields):
        begin = upwind(left_ref[f], my_left[f], u0)
        end = upwind(my_right[f], right_ref[f], u16)
        row_m1[f] = left_ref[fields + f] - begin
        row_0[f] = my_left[fields + f] + begin
        lo = my_right[fields + f] - end
        hi = right_ref[fields + f] + end
        row_15[f] = lo
        speed = gain * (hi - lo) * inverse(hi + lo)
        flux_16[f] = upwind(lo, hi, speed)

    def body(l, c):
        u = cour_ref[0, l]
        v = cour_ref[1, l] * wall
        gain_x = jnp.abs(u) - u * u
        gain_y = jnp.abs(v) - v * v
        one = pl.ds(l, 1)
        for f in range(fields):
            p = first_ref[f, l]
            p = jnp.where(is_first, row_0[f, one, :], jnp.where(is_last, row_15[f, one, :], p))
            lo = jnp.where(is_first, row_m1[f, one, :], pltpu.roll(p, 1, 0))
            flux = upwind(lo, p, gain_x * (p - lo) * inverse(p + lo))
            lo = pltpu.roll(p, 1, 1)
            flux_y = upwind(lo, p, gain_y * (p - lo) * inverse(p + lo))
            beyond = jnp.where(is_last, flux_16[f, one, :], pltpu.roll(flux, last, 0))
            out_ref[f, l] = p - (beyond - flux) - (pltpu.roll(flux_y, cells_y - 1, 1) - flux_y)
        return c

    lax.fori_loop(0, block, body, 0, unroll=TWO_UNROLL)


def pass_two(first, courant, my_right, my_left, left, right):
    fields, levels, cells_x, cells_y = first.shape
    block = TWO_BLOCK
    plane = pl.BlockSpec((fields, block, cells_x, cells_y), lambda i: (0, i, 0, 0))
    rows = pltpu.VMEM((fields, block, cells_y), jnp.float32)
    return pl.pallas_call(
        pass_two_kernel,
        grid=(levels // block,),
        in_specs=[
            plane,
            pl.BlockSpec((2, block, cells_x, cells_y), lambda i: (0, i, 0, 0)),
        ]
        + [
            pl.BlockSpec((edge.shape[0], block, cells_y), lambda i: (0, i, 0))
            for edge in (my_right, my_left, left, right)
        ],
        out_specs=plane,
        out_shape=jax.ShapeDtypeStruct(first.shape, jnp.float32),
        scratch_shapes=[rows, rows, rows, rows],
        compiler_params=pltpu.CompilerParams(vmem_limit_bytes=SMALL_VMEM),
        name="pass_two",
    )(first, courant, my_right, my_left, left, right)


def warm_kernel(field_ref, heat_ref, out_ref):
    block = field_ref.shape[1]
    start = pl.program_id(0) * block

    def body(l, c):
        for xh in range(2):
            for yh in range(2):
                part = (0, l, slice(8 * xh, 8 * xh + 8), slice(128 * yh, 128 * yh + 128))
                heating = spread_row(heat_ref, start + l, xh, yh)
                out_ref[part] = field_ref[part] + STEP_LENGTH * heating
        return c

    lax.fori_loop(0, block, body, 0, unroll=WARM_UNROLL)


def warm(fields, heat):
    _, levels, cells_x, cells_y = fields.shape
    block = WARM_BLOCK
    spec = pl.BlockSpec((1, block, cells_x, cells_y), lambda i: (0, i, 0, 0))
    return pl.pallas_call(
        warm_kernel,
        grid=(levels // block,),
        in_specs=[spec, pl.BlockSpec(memory_space=pltpu.VMEM)],
        out_specs=spec,
        out_shape=jax.ShapeDtypeStruct(fields.shape, jnp.float32),
        input_output_aliases={0: 0},
        compiler_params=pltpu.CompilerParams(vmem_limit_bytes=SMALL_VMEM),
        name="warm",
    )(fields, heat)


def per_device(prognostic, courant, daylit, cos_zenith, albedo, *optics):
    dynamics = lax.axis_index("grp") == 0
    tiles = lax.axis_size("tile")
    to_right, to_left = lax.cond(
        dynamics, lambda: edges(prognostic, courant), lambda: no_edges(prognostic)
    )
    left = lax.ppermute(to_right, ("grp", "tile"), [(i, (i + 1) % tiles) for i in range(tiles)])
    right = lax.ppermute(to_left, ("grp", "tile"), [((i + 1) % tiles, i) for i in range(tiles)])
    first, heat, fluxes = lax.cond(
        dynamics,
        lambda: pass_one(prognostic, courant),
        lambda: radiation(prognostic, daylit, cos_zenith, albedo, optics),
    )
    heat_in = lax.ppermute(heat, "grp", [(1, 0)])
    fields = lax.cond(
        dynamics,
        lambda left, right: pass_two(first, courant, to_right, to_left, left, right),
        lambda left, right: expand(daylit, heat, fluxes, prognostic.shape),
        left, right,
    )
    return warm(fields, heat_in)[None]


def solution(mesh):
    column = P("tile")
    plane = P(None, None, "tile", None)
    return jax.shard_map(
        per_device,
        mesh=mesh,
        in_specs=(plane, plane, column, column, column) + (P(),) * 6,
        out_specs=P("grp", None, None, "tile", None),
        check_vma=False,
    )
```

```python
import functools

import jax
import jax.numpy as jnp
from jax import lax
from jax.experimental import pallas as pl
from jax.experimental.pallas import tpu as pltpu
from jax.sharding import PartitionSpec as P

COARSEN = 4
DIFFUSIVITY = 1.66
STEP_LENGTH = 1.0
LOG2E = 1.4426950408889634
G_CHUNK = 8
UP_UNROLL = 8
DOWN_UNROLL = 4
EDGE_BLOCK = 32
ONE_BLOCK = 16
ONE_UNROLL = 4
TWO_BLOCK = 32
TWO_UNROLL = 4
EXPAND_BLOCK = 16
WARM_BLOCK = 32
WARM_UNROLL = 8
COARSE_UNROLL = 8
COARSE_CHUNKS = 4
SOLVE_VMEM = 24 * 1024 * 1024
SMALL_VMEM = 16 * 1024 * 1024


def pack_means(tile):
    sub = lax.broadcasted_iota(jnp.int32, (8, 128), 0) % 4
    packed = None
    for xh in range(2):
        for yh in range(2):
            part = tile[8 * xh : 8 * xh + 8, 128 * yh : 128 * yh + 128]
            part = part + pltpu.roll(part, 7, 0)
            part = part + pltpu.roll(part, 6, 0)
            k = 2 * xh + yh
            if k:
                part = pltpu.roll(part, k, 0)
            packed = part if packed is None else jnp.where(sub == k, part, packed)
    return packed * (1.0 / COARSEN)


def spread_part(packed, xh, yh):
    k = 2 * xh + yh
    low = jnp.broadcast_to(packed[k : k + 1], (8, 128))
    high = jnp.broadcast_to(packed[4 + k : 5 + k], (8, 128))
    return jnp.where(lax.broadcasted_iota(jnp.int32, (8, 128), 0) < 4, low, high)


def spread_row(ref, l, xh, yh):
    k = 2 * xh + yh
    low = jnp.broadcast_to(ref[l, k : k + 1, :], (8, 128))
    high = jnp.broadcast_to(ref[l, 4 + k : 5 + k, :], (8, 128))
    return jnp.where(lax.broadcasted_iota(jnp.int32, (8, 128), 0) < 4, low, high)


def register_order(rows):
    return jnp.concatenate([rows[0:2], rows[4:6], rows[2:4], rows[6:8]], axis=0)


def radiation_kernel(
    mass_s, vap_s, oz_s, ext_s, alb_s, sol_s,
    lit_ref, cos_ref, ground_ref, prog_ref,
    unused_ref, heat_ref, acc,
    fine, sems, coarse, k_tdir, k_a, k_b, k_ad, k_as,
):
    chunk = pl.program_id(0)
    levels = acc.shape[1]

    @pl.when(chunk == 0)
    def _():
        part = levels // COARSE_CHUNKS
        copies = []
        for c in range(COARSE_CHUNKS):
            here = pl.ds(c * part, part)
            copies.append(
                pltpu.make_async_copy(prog_ref.at[pl.ds(1, 3), here], fine.at[:, here], sems.at[c])
            )
            copies[-1].start()

        def body(l, c):
            scale = mass_s[l]
            for f in range(3):
                coarse[f, l] = pack_means(fine[f, l]) * scale
            for f in range(4):
                acc[f, l] = jnp.zeros((8, 128), jnp.float32)
            return c

        for c in range(COARSE_CHUNKS):
            copies[c].wait()
            lax.fori_loop(c * part, (c + 1) * part, body, 0, unroll=COARSE_UNROLL)

    cosine = register_order(cos_ref[...])
    ground = register_order(ground_ref[...])
    dir_rate = -LOG2E / cosine
    dif_rate = -LOG2E * DIFFUSIVITY
    g0 = chunk * G_CHUNK
    oz = [oz_s[g0 + j] for j in range(G_CHUNK)]
    ext = [ext_s[g0 + j] for j in range(G_CHUNK)]
    half_alb = [0.5 * alb_s[g0 + j] for j in range(G_CHUNK)]

    def upward(i, carry):
        l = levels - 1 - i
        alb_dif, alb_dir = carry
        vapour, cloud, ozone = coarse[0, l], coarse[1, l], coarse[2, l]
        new_dif, new_dir = [], []
        for j in range(G_CHUNK):
            cloud_depth = cloud * ext[j]
            depth = (vapour * vap_s[l, g0 + j] + ozone * oz[j]) + cloud_depth
            half_w = (cloud_depth * half_alb[j]) * inverse(depth)
            t_dir = jnp.exp2(depth * dir_rate)
            t_dif = jnp.exp2(depth * dif_rate)
            t_sq = t_dif * t_dif
            r_dif = half_w * (1.0 - t_sq)
            s_dir = half_w * (1.0 - t_dir)
            den = inverse(1.0 - r_dif * alb_dif[j])
            through = alb_dir[j] * t_dir
            down = (s_dir + r_dif * through) * den
            k_tdir[l, j] = t_dir
            k_a[l, j] = t_dif * den
            k_b[l, j] = down
            k_ad[l, j] = alb_dif[j]
            k_as[l, j] = alb_dir[j]
            new_dir.append(s_dir + t_dif * (alb_dif[j] * down + through))
            new_dif.append(r_dif + t_sq * alb_dif[j] * den)
        return tuple(new_dif), tuple(new_dir)

    start = (ground,) * G_CHUNK
    _, top_dir = lax.fori_loop(0, levels, upward, (start, start), unroll=UP_UNROLL)

    direct0 = tuple(cosine * sol_s[g0 + j] for j in range(G_CHUNK))
    net0 = tuple(d - t * d for d, t in zip(direct0, top_dir))
    diffuse0 = tuple(jnp.zeros((8, 128), jnp.float32) for _ in range(G_CHUNK))

    def downward(l, carry):
        direct, diffuse, net = carry
        n_direct, n_diffuse, n_net = [], [], []
        sums = None
        for j in range(G_CHUNK):
            s_low = direct[j] * k_tdir[l, j]
            d_low = diffuse[j] * k_a[l, j] + direct[j] * k_b[l, j]
            up = k_ad[l, j] * d_low + k_as[l, j] * s_low
            total = s_low + d_low
            low_net = total - up
            terms = (net[j] - low_net, total, up, s_low)
            sums = terms if sums is None else tuple(a + b for a, b in zip(sums, terms))
            n_direct.append(s_low)
            n_diffuse.append(d_low)
            n_net.append(low_net)
        for f in range(4):
            acc[f, l] += sums[f]
        return tuple(n_direct), tuple(n_diffuse), tuple(n_net)

    lax.fori_loop(0, levels, downward, (direct0, diffuse0, net0), unroll=DOWN_UNROLL)

    @pl.when(chunk == pl.num_programs(0) - 1)
    def _():
        lit = register_order(lit_ref[...]).astype(jnp.float32)

        def body(l, c):
            heat_ref[l] = acc[0, l] * lit * (float(levels) / jnp.full((8, 128), mass_s[l]))
            return c

        lax.fori_loop(0, levels, body, 0, unroll=4)


def radiation(prognostic, daylit, cos_zenith, albedo, optics):
    fields, levels, cells_x, cells_y = prognostic.shape
    g_points = optics[1].shape[1]
    smem = pl.BlockSpec(memory_space=pltpu.SMEM)
    vec = pl.BlockSpec((8, 128), lambda c: (0, 0))
    kept = pltpu.VMEM((levels, G_CHUNK, 8, 128), jnp.float32)
    return pl.pallas_call(
        radiation_kernel,
        grid=(g_points // G_CHUNK,),
        in_specs=[smem] * 6 + [vec] * 3 + [pl.BlockSpec(memory_space=pl.ANY)],
        out_specs=[
            pl.BlockSpec(memory_space=pl.ANY),
            pl.BlockSpec((levels, 8, 128), lambda c: (0, 0, 0)),
            pl.BlockSpec((4, levels, 8, 128), lambda c: (0, 0, 0, 0)),
        ],
        out_shape=[
            jax.ShapeDtypeStruct(prognostic.shape, jnp.float32),
            jax.ShapeDtypeStruct((levels, 8, 128), jnp.float32),
            jax.ShapeDtypeStruct((4, levels, 8, 128), jnp.float32),
        ],
        scratch_shapes=[
            pltpu.VMEM((3, levels, cells_x, cells_y), jnp.float32),
            pltpu.SemaphoreType.DMA((COARSE_CHUNKS,)),
            pltpu.VMEM((3, levels, 8, 128), jnp.float32),
            kept, kept, kept, kept, kept,
        ],
        compiler_params=pltpu.CompilerParams(vmem_limit_bytes=SOLVE_VMEM),
        name="radiation",
    )(
        *optics,
        daylit.reshape(8, 128), cos_zenith.reshape(8, 128), albedo.reshape(8, 128),
        prognostic,
    )


def expand_kernel(lit_ref, heat_ref, acc_ref, out_ref):
    lit = register_order(lit_ref[...]).astype(jnp.float32)

    def body(l, c):
        for f in range(4):
            value = heat_ref[l] if f == 0 else acc_ref[f, l] * lit
            for xh in range(2):
                for yh in range(2):
                    out_ref[f, l, 8 * xh : 8 * xh + 8, 128 * yh : 128 * yh + 128] = spread_part(
                        value, xh, yh
                    )
        return c

    lax.fori_loop(0, heat_ref.shape[0], body, 0, unroll=2)


def expand(daylit, heat, fluxes, shape):
    fields, levels, cells_x, cells_y = shape
    block = EXPAND_BLOCK
    return pl.pallas_call(
        expand_kernel,
        grid=(levels // block,),
        in_specs=[
            pl.BlockSpec((8, 128), lambda i: (0, 0)),
            pl.BlockSpec((block, 8, 128), lambda i: (i, 0, 0)),
            pl.BlockSpec((4, block, 8, 128), lambda i: (0, i, 0, 0)),
        ],
        out_specs=pl.BlockSpec((fields, block, cells_x, cells_y), lambda i: (0, i, 0, 0)),
        out_shape=jax.ShapeDtypeStruct(shape, jnp.float32),
        compiler_params=pltpu.CompilerParams(vmem_limit_bytes=SMALL_VMEM),
        name="expand",
    )(daylit.reshape(8, 128), heat, fluxes)


def inverse(value):
    return pl.reciprocal(value, approx=False)


def wall_mask(shape):
    return (lax.broadcasted_iota(jnp.int32, shape, len(shape) - 1) > 0).astype(jnp.float32)


def upwind(low, high, face):
    return jnp.maximum(face, 0.0) * low + jnp.minimum(face, 0.0) * high


def across_y(value, face):
    flux = upwind(pltpu.roll(value, 1, 1), value, face)
    return pltpu.roll(flux, value.shape[1] - 1, 1) - flux


def edges_kernel(prog_ref, cour_ref, right_ref, left_ref, rows):
    fields, block, cells_x, cells_y = prog_ref.shape
    last = cells_x - 1
    picks = [(prog_ref, f, x) for x in (last, last - 1, 0, 1) for f in range(fields)]
    picks += [(cour_ref, 0, last), (cour_ref, 0, 1), (cour_ref, 0, 0), (cour_ref, 1, last), (cour_ref, 1, 0)]
    for l in range(block):
        for k, (ref, f, x) in enumerate(picks):
            rows[k, l : l + 1, :] = ref[f, l, x : x + 1, :]
    base = 4 * fields
    u_last, u_one, u_zero = rows[base], rows[base + 1], rows[base + 2]
    wall = wall_mask((block, cells_y))
    v_last, v_zero = rows[base + 3] * wall, rows[base + 4] * wall
    for f in range(fields):
        end, inner = rows[f], rows[fields + f]
        right_ref[f] = end
        right_ref[fields + f] = end + upwind(inner, end, u_last) - across_y(end, v_last)
        start, inner = rows[2 * fields + f], rows[3 * fields + f]
        left_ref[f] = start
        left_ref[fields + f] = start - upwind(start, inner, u_one) - across_y(start, v_zero)
    left_ref[2 * fields] = u_zero


def edges(prognostic, courant):
    fields, levels, cells_x, cells_y = prognostic.shape
    block = EDGE_BLOCK
    return pl.pallas_call(
        edges_kernel,
        grid=(levels // block,),
        in_specs=[
            pl.BlockSpec((fields, block, cells_x, cells_y), lambda i: (0, i, 0, 0)),
            pl.BlockSpec((2, block, cells_x, cells_y), lambda i: (0, i, 0, 0)),
        ],
        out_specs=[
            pl.BlockSpec((2 * fields, block, cells_y), lambda i: (0, i, 0)),
            pl.BlockSpec((2 * fields + 1, block, cells_y), lambda i: (0, i, 0)),
        ],
        out_shape=[
            jax.ShapeDtypeStruct((2 * fields, levels, cells_y), jnp.float32),
            jax.ShapeDtypeStruct((2 * fields + 1, levels, cells_y), jnp.float32),
        ],
        scratch_shapes=[pltpu.VMEM((4 * fields + 5, block, cells_y), jnp.float32)],
        compiler_params=pltpu.CompilerParams(vmem_limit_bytes=SMALL_VMEM),
        name="edges",
    )(prognostic, courant)


def no_edges(prognostic):
    fields, levels, _, cells_y = prognostic.shape
    return pl.pallas_call(
        lambda right_ref, left_ref: None,
        out_specs=[pl.BlockSpec(memory_space=pl.ANY)] * 2,
        out_shape=[
            jax.ShapeDtypeStruct((2 * fields, levels, cells_y), jnp.float32),
            jax.ShapeDtypeStruct((2 * fields + 1, levels, cells_y), jnp.float32),
        ],
        compiler_params=pltpu.CompilerParams(vmem_limit_bytes=SMALL_VMEM),
        name="no_edges",
    )()


def pass_one_kernel(prog_ref, cour_ref, first_ref, heat_ref, acc_ref):
    fields, block, cells_x, cells_y = prog_ref.shape
    shape = (cells_x, cells_y)
    wall = wall_mask(shape)
    inside = (lax.broadcasted_iota(jnp.int32, shape, 0) > 0).astype(jnp.float32)

    def body(l, c):
        u = cour_ref[0, l] * inside
        v = cour_ref[1, l] * wall
        up, um = jnp.maximum(u, 0.0), jnp.minimum(u, 0.0)
        vp, vm = jnp.maximum(v, 0.0), jnp.minimum(v, 0.0)
        for f in range(fields):
            p = prog_ref[f, l]
            flux = up * pltpu.roll(p, 1, 0) + um * p
            flux_y = vp * pltpu.roll(p, 1, 1) + vm * p
            first_ref[f, l] = (
                p
                - (pltpu.roll(flux, cells_x - 1, 0) - flux)
                - (pltpu.roll(flux_y, cells_y - 1, 1) - flux_y)
            )
        return c

    lax.fori_loop(0, block, body, 0, unroll=ONE_UNROLL)


def pass_one(prognostic, courant):
    fields, levels, cells_x, cells_y = prognostic.shape
    block = ONE_BLOCK
    plane = pl.BlockSpec((fields, block, cells_x, cells_y), lambda i: (0, i, 0, 0))
    return pl.pallas_call(
        pass_one_kernel,
        grid=(levels // block,),
        in_specs=[plane, pl.BlockSpec((2, block, cells_x, cells_y), lambda i: (0, i, 0, 0))],
        out_specs=[plane, pl.BlockSpec(memory_space=pl.ANY), pl.BlockSpec(memory_space=pl.ANY)],
        out_shape=[
            jax.ShapeDtypeStruct(prognostic.shape, jnp.float32),
            jax.ShapeDtypeStruct((levels, 8, 128), jnp.float32),
            jax.ShapeDtypeStruct((4, levels, 8, 128), jnp.float32),
        ],
        compiler_params=pltpu.CompilerParams(vmem_limit_bytes=SMALL_VMEM),
        name="pass_one",
    )(prognostic, courant)


def pass_two_kernel(
    first_ref, cour_ref, my_right, my_left, left_ref, right_ref,
    out_ref, row_m1, row_0, row_15, flux_16,
):
    fields, block, cells_x, cells_y = first_ref.shape
    shape = (cells_x, cells_y)
    last = cells_x - 1
    row = lax.broadcasted_iota(jnp.int32, shape, 0)
    wall = wall_mask(shape)
    is_first, is_last = row == 0, row == last

    u0, u16 = my_left[2 * fields], right_ref[2 * fields]
    gain = jnp.abs(u16) - u16 * u16
    for f in range(fields):
        begin = upwind(left_ref[f], my_left[f], u0)
        end = upwind(my_right[f], right_ref[f], u16)
        row_m1[f] = left_ref[fields + f] - begin
        row_0[f] = my_left[fields + f] + begin
        lo = my_right[fields + f] - end
        hi = right_ref[fields + f] + end
        row_15[f] = lo
        speed = gain * (hi - lo) * inverse(hi + lo)
        flux_16[f] = upwind(lo, hi, speed)

    def body(l, c):
        u = cour_ref[0, l]
        v = cour_ref[1, l] * wall
        gain_x = jnp.abs(u) - u * u
        gain_y = jnp.abs(v) - v * v
        one = pl.ds(l, 1)
        for f in range(fields):
            p = first_ref[f, l]
            p = jnp.where(is_first, row_0[f, one, :], jnp.where(is_last, row_15[f, one, :], p))
            lo = jnp.where(is_first, row_m1[f, one, :], pltpu.roll(p, 1, 0))
            flux = upwind(lo, p, gain_x * (p - lo) * inverse(p + lo))
            lo = pltpu.roll(p, 1, 1)
            flux_y = upwind(lo, p, gain_y * (p - lo) * inverse(p + lo))
            beyond = jnp.where(is_last, flux_16[f, one, :], pltpu.roll(flux, last, 0))
            out_ref[f, l] = p - (beyond - flux) - (pltpu.roll(flux_y, cells_y - 1, 1) - flux_y)
        return c

    lax.fori_loop(0, block, body, 0, unroll=TWO_UNROLL)


def pass_two(first, courant, my_right, my_left, left, right):
    fields, levels, cells_x, cells_y = first.shape
    block = TWO_BLOCK
    plane = pl.BlockSpec((fields, block, cells_x, cells_y), lambda i: (0, i, 0, 0))
    rows = pltpu.VMEM((fields, block, cells_y), jnp.float32)
    return pl.pallas_call(
        pass_two_kernel,
        grid=(levels // block,),
        in_specs=[
            plane,
            pl.BlockSpec((2, block, cells_x, cells_y), lambda i: (0, i, 0, 0)),
        ]
        + [
            pl.BlockSpec((edge.shape[0], block, cells_y), lambda i: (0, i, 0))
            for edge in (my_right, my_left, left, right)
        ],
        out_specs=plane,
        out_shape=jax.ShapeDtypeStruct(first.shape, jnp.float32),
        scratch_shapes=[rows, rows, rows, rows],
        compiler_params=pltpu.CompilerParams(vmem_limit_bytes=SMALL_VMEM),
        name="pass_two",
    )(first, courant, my_right, my_left, left, right)


def warm_kernel(field_ref, heat_ref, out_ref):
    block = field_ref.shape[1]
    start = pl.program_id(0) * block

    def body(l, c):
        for xh in range(2):
            for yh in range(2):
                part = (0, l, slice(8 * xh, 8 * xh + 8), slice(128 * yh, 128 * yh + 128))
                heating = spread_row(heat_ref, start + l, xh, yh)
                out_ref[part] = field_ref[part] + STEP_LENGTH * heating
        return c

    lax.fori_loop(0, block, body, 0, unroll=WARM_UNROLL)


def warm(fields, heat):
    _, levels, cells_x, cells_y = fields.shape
    block = WARM_BLOCK
    spec = pl.BlockSpec((1, block, cells_x, cells_y), lambda i: (0, i, 0, 0))
    return pl.pallas_call(
        warm_kernel,
        grid=(levels // block,),
        in_specs=[spec, pl.BlockSpec(memory_space=pltpu.VMEM)],
        out_specs=spec,
        out_shape=jax.ShapeDtypeStruct(fields.shape, jnp.float32),
        input_output_aliases={0: 0},
        compiler_params=pltpu.CompilerParams(vmem_limit_bytes=SMALL_VMEM),
        name="warm",
    )(fields, heat)


def per_device(prognostic, courant, daylit, cos_zenith, albedo, *optics):
    dynamics = lax.axis_index("grp") == 0
    tiles = lax.axis_size("tile")
    to_right, to_left = lax.cond(
        dynamics, lambda: edges(prognostic, courant), lambda: no_edges(prognostic)
    )
    left = lax.ppermute(to_right, ("grp", "tile"), [(i, (i + 1) % tiles) for i in range(tiles)])
    right = lax.ppermute(to_left, ("grp", "tile"), [((i + 1) % tiles, i) for i in range(tiles)])
    first, heat, fluxes = lax.cond(
        dynamics,
        lambda: pass_one(prognostic, courant),
        lambda: radiation(prognostic, daylit, cos_zenith, albedo, optics),
    )
    heat_in = lax.ppermute(heat, "grp", [(1, 0)])
    fields = lax.cond(
        dynamics,
        lambda left, right: pass_two(first, courant, to_right, to_left, left, right),
        lambda left, right: expand(daylit, heat, fluxes, prognostic.shape),
        left, right,
    )
    return warm(fields, heat_in)[None]


def solution(mesh):
    column = P("tile")
    plane = P(None, None, "tile", None)
    return jax.shard_map(
        per_device,
        mesh=mesh,
        in_specs=(plane, plane, column, column, column) + (P(),) * 6,
        out_specs=P("grp", None, None, "tile", None),
        check_vma=False,
    )
```
